512 devices in a mesh: wide: 32 (over z_hi, x, core), blk: 16 (over z_lo, y).
Axes of the slice: x: 4, y: 4, z: 16 (z_hi: 4, z_lo: 4; z = z_hi * 4 + z_lo), core: 2. Of those that a mesh axis runs over, the one named last changes fastest.
Arguments:
- sources: bfloat16 [512, 64000], P(('wide', 'blk')), may hold values from -6 to 6
- targets: bfloat16 [16, 64000], P('blk'), may hold values from -6 to 6
Outputs:
- exchange_field: float32 [16, 64000], P('blk', 'wide')
The draws below stay inside these ranges and needn't reach their ends.
All inputs are finite; a program needn't handle non-finite values.
Results may differ from the reference program's by a relative error of at most 0.014.
Values may be sent and summed in bfloat16 or wider, within the bound.
No kernel may reach another device: no remote copies, remote signals or barrier semaphores. Data moves between devices by JAX's collectives and lax.ppermute only.
A program may use at most 64 MiB of HBM per device.

```python
import math
import jax
import jax.numpy as jnp
from jax import lax

GRID = 40
SRC_DEV = 1
HOPS = 2
CELLS = 64000
SOURCES = 512
TARGETS = 16
N_WIDE = 32
N_BLK = 16


def spiked(drawn, stream_key, source, target, shards_of, factor):
    owner, partner = [(jnp.arange(drawn.shape[axis_at]) // (drawn.shape[axis_at] // shards_of)).reshape([-1 if axis == axis_at else 1 for axis in range(drawn.ndim)]) for axis_at in (source, target)]
    chosen = jax.random.permutation(stream_key, shards_of)[partner]
    strong = (owner == chosen) | (owner == (partner + shards_of // 2) % shards_of)
    return jnp.where(strong, factor * drawn, drawn)


def level_of(key, dims, shards, low, top_value):
    level = 1.0
    for axis_at, blocks in shards:
        steps = jax.random.uniform(jax.random.fold_in(jax.random.fold_in(key, 6), axis_at), (blocks,), jnp.float32, low / len(shards), top_value / len(shards))
        level = level * jnp.repeat(jnp.exp(steps), dims[axis_at] // blocks).reshape((-1,) + (1,) * (len(dims) - 1 - axis_at))
    return level


def scatter_about(key, shape, spread, most, shards=(), kind=jnp.bfloat16):
    loudness = level_of(key, shape, shards, -0.22, 0.18) if shards else 1.0
    entries = jax.random.normal(key, shape, jnp.float32) * spread * loudness
    return jnp.minimum(jnp.maximum(entries, -most), most).astype(kind)


def noise_with(key, shape, scale, limit, cuts, heavy, kind=jnp.bfloat16):
    entries = scale * jax.random.normal(key, shape, jnp.float32)
    if cuts:
        entries = entries * level_of(key, shape, cuts, -0.22, 0.18)
    return jnp.clip(spiked(entries, jax.random.fold_in(key, 3), *heavy), -limit, limit).astype(kind)


def setup_inputs(seed: int = 0) -> dict:
    key_of = jax.random.split(jax.random.key(seed), 3)
    sources = noise_with(key_of[0], (SOURCES, CELLS), (HOPS * N_WIDE // 4) ** -0.5, 6.0, ((0, 512),), (0, 1, 512, 6.0))
    targets = scatter_about(key_of[1], (TARGETS, CELLS), 1.0, 6.0, ((0, 16),))
    return {"sources": sources, "targets": targets}


screen = 0.3


def tables(grid):
    index = jnp.arange(grid, dtype=jnp.int32)
    product = (index[:, None] * index[None, :]) % grid
    angle = (2.0 * math.pi / grid) * product.astype(jnp.float32)
    return jnp.concatenate([jnp.cos(angle), jnp.sin(angle)], axis=0).astype(jnp.bfloat16)


def kernel_table(grid):
    index = jnp.arange(grid, dtype=jnp.int32)
    wrapped = ((index + grid // 2) % grid) - grid // 2
    wave = (2.0 * math.pi / grid) * wrapped.astype(jnp.float32)
    square = wave * wave
    total = square[:, None, None] + square[None, :, None] + square[None, None, :]
    values = (4.0 * math.pi) / (total + screen * screen) / float(grid ** 3)
    return values.reshape(grid, grid * grid)


def turn(field, both):
    width = both.shape[1]
    cos_table = both[:width].astype(jnp.float32)
    sin_table = both[width:].astype(jnp.float32)
    wide_field = field.astype(jnp.float32)
    cpart = jnp.einsum("mnr,kn->mrk", wide_field, cos_table, precision=lax.Precision.HIGHEST)
    spart = jnp.einsum("mnr,kn->mrk", wide_field, sin_table, precision=lax.Precision.HIGHEST)
    return cpart.reshape(field.shape), spart.reshape(field.shape)


def potential(pair, both, kern):
    cpart, spart = turn(pair, both)
    real_part = cpart.astype(jnp.bfloat16)
    imag_part = (-spart).astype(jnp.bfloat16)
    for section in range(2):
        rcos, rsin = turn(real_part, both)
        icos, isin = turn(imag_part, both)
        new_real = rcos + isin
        new_imag = icos - rsin
        if section == 1:
            new_real = new_real * kern
            new_imag = new_imag * kern
        real_part = new_real.astype(jnp.bfloat16)
        imag_part = new_imag.astype(jnp.bfloat16)
    for section in range(2):
        rcos, rsin = turn(real_part, both)
        icos, isin = turn(imag_part, both)
        real_part = (rcos - isin).astype(jnp.bfloat16)
        imag_part = (icos + rsin).astype(jnp.bfloat16)
    rcos, rsin = turn(real_part, both)
    icos, isin = turn(imag_part, both)
    return rcos - isin


def exchange_term(chosen, target, both, kern):
    grid = both.shape[1]
    count = chosen.shape[0]
    pair = (chosen.astype(jnp.float32) * target.astype(jnp.float32)[None, :]).astype(jnp.bfloat16)
    pair = pair.reshape(count, grid, grid * grid)
    field = potential(pair, both, kern).reshape(count, grid ** 3)
    return -jnp.sum(chosen.astype(jnp.float32) * field, axis=0)


def reference(sources, targets):
    both = tables(GRID)
    kern = kernel_table(GRID)
    blocks = sources.reshape(N_WIDE, N_BLK, SRC_DEV, CELLS)

    def one_row(row):
        owner = ((row - HOPS + 1) % N_BLK).astype(jnp.int32)
        picks = ((owner + jnp.arange(HOPS, dtype=jnp.int32)) % N_BLK).astype(jnp.int32)
        chosen = jnp.take(blocks, picks, axis=1).reshape(N_WIDE * HOPS * SRC_DEV, CELLS)
        target = lax.dynamic_index_in_dim(targets, owner, 0, keepdims=False)
        return exchange_term(chosen, target, both, kern)

    return lax.map(one_row, jnp.arange(N_BLK, dtype=jnp.int32))
```

```python
import functools
import math

import jax
import jax.numpy as jnp
import numpy as np
from jax import lax
from jax.experimental import pallas as pl
from jax.experimental.pallas import tpu as pltpu
from jax.sharding import PartitionSpec as P

GRID = 40
ROWS = GRID * GRID
LANES = 128
HALF = 64
PIECES = 32
PIECE = GRID**3 // PIECES
GROUPS = PIECE // GRID
SCREEN = 0.3


def tables():
    index = np.arange(GRID)
    product = index[:, None] * index[None, :] % GRID
    folded = np.minimum(product, GRID - product)
    angle = 2.0 * math.pi / GRID * folded
    cos = np.cos(angle)
    sin = np.where(product <= GRID // 2, 1.0, -1.0) * np.sin(angle)
    sin = np.where((product == 0) | (product == GRID // 2), 0.0, sin)
    return cos.astype(np.float32), sin.astype(np.float32)


def weights():
    cos, sin = tables()
    left = np.concatenate([cos, sin], axis=1)

    def right(sign):
        out = np.zeros((LANES, LANES), np.float32)
        out[:GRID, :GRID] = cos
        out[:GRID, HALF : HALF + GRID] = -sign * sin
        out[HALF : HALF + GRID, :GRID] = sign * sin
        out[HALF : HALF + GRID, HALF : HALF + GRID] = cos
        return out

    return left, right(1.0), right(-1.0)


def kernel_table():
    index = jnp.arange(GRID, dtype=jnp.int32)
    wrapped = (index + GRID // 2) % GRID - GRID // 2
    wave = 2.0 * math.pi / GRID * wrapped.astype(jnp.float32)
    square = wave * wave
    lane = jnp.arange(LANES, dtype=jnp.int32) % HALF
    lane_wrapped = (lane + GRID // 2) % GRID - GRID // 2
    lane_wave = 2.0 * math.pi / GRID * lane_wrapped.astype(jnp.float32)
    lane_square = lane_wave * lane_wave
    total = square[None, :, None] + square[:, None, None] + lane_square[None, None, :]
    return 4.0 * math.pi / (total + SCREEN * SCREEN) / float(GRID**3)


def body(s0_ref, s1_ref, t_ref, kern_ref, left_ref, fwd_ref, inv_ref, out_ref, xs, flat):
    lane = lax.broadcasted_iota(jnp.int32, (PIECES, LANES), 1)
    low = lane < HALF
    wide = flat.shape[2]

    target = t_ref[...].astype(jnp.float32)
    flat[0, :, :PIECE] = s0_ref[...].astype(jnp.float32) * target
    flat[1, :, :PIECE] = s1_ref[...].astype(jnp.float32) * target
    flat[:, :, PIECE:] = jnp.zeros((2, PIECES, wide - PIECE), jnp.float32)

    def aligned(which, group, to):
        start = GRID * group
        tile, shift = start // LANES, start % LANES
        value = flat[which, :, tile * LANES : (tile + 1) * LANES]
        if shift + GRID > LANES:
            after = flat[which, :, (tile + 1) * LANES : (tile + 2) * LANES]
            value = jnp.where(lane >= shift, value, after)
        turn = (to - shift) % LANES
        return pltpu.roll(value, turn, 1) if turn else value

    for group in range(GROUPS):
        merged = jnp.where(low, aligned(0, group, 0), aligned(1, group, HALF))
        xs[pl.ds(group, PIECES, stride=GROUPS), :] = merged

    left = left_ref[...]
    slab_lane = lax.broadcasted_iota(jnp.int32, (GRID, LANES), 1)
    forward_sign = jnp.where(slab_lane < HALF, 1.0, -1.0).astype(jnp.float32)

    def stacked(slab, sign):
        return jnp.concatenate([slab, pltpu.roll(slab, HALF, 1) * sign], axis=0)

    def left_turn(first, second, sign):
        both = jnp.concatenate([stacked(first, sign), stacked(second, sign)], axis=1)
        return jnp.dot(left, both.astype(jnp.bfloat16), preferred_element_type=jnp.float32)

    def along_b(sign):
        for pair in range(GRID // 2):
            one, two = pl.ds(2 * pair * GRID, GRID), pl.ds((2 * pair + 1) * GRID, GRID)
            turned = left_turn(xs[one, :], xs[two, :], sign)
            xs[one, :] = turned[:, :LANES]
            xs[two, :] = turned[:, LANES:]

    xs[...] = jnp.dot(xs[...].astype(jnp.bfloat16), fwd_ref[...], preferred_element_type=jnp.float32)
    along_b(forward_sign)
    for pair in range(GRID // 2):
        one, two = pl.ds(2 * pair, GRID, stride=GRID), pl.ds(2 * pair + 1, GRID, stride=GRID)
        turned = left_turn(xs[one, :], xs[two, :], forward_sign)
        first = turned[:, :LANES] * kern_ref[2 * pair]
        second = turned[:, LANES:] * kern_ref[2 * pair + 1]
        turned = left_turn(first, second, -forward_sign)
        xs[one, :] = turned[:, :LANES]
        xs[two, :] = turned[:, LANES:]
    along_b(-forward_sign)
    xs[...] = jnp.dot(xs[...].astype(jnp.bfloat16), inv_ref[...], preferred_element_type=jnp.float32)

    tiles = [[None] * (wide // LANES) for _ in range(2)]
    for group in range(GROUPS):
        start = GRID * group
        tile, shift = start // LANES, start % LANES
        value = xs[pl.ds(group, PIECES, stride=GROUPS), :]
        for which in range(2):
            turn = (shift - HALF * which) % LANES
            moved = pltpu.roll(value, turn, 1) if turn else value
            held = tiles[which][tile]
            tiles[which][tile] = moved if held is None else jnp.where(lane >= shift, moved, held)
            if shift + GRID > LANES:
                tiles[which][tile + 1] = moved
    for tile in range(wide // LANES):
        size = min(LANES, PIECE - tile * LANES)
        here = slice(tile * LANES, tile * LANES + size)
        total = s0_ref[:, here].astype(jnp.float32) * tiles[0][tile][:, :size]
        total += s1_ref[:, here].astype(jnp.float32) * tiles[1][tile][:, :size]
        out_ref[:, here] = (-total).astype(jnp.bfloat16)


def exchange_term(s0, s1, target):
    left, fwd, inv = (jnp.asarray(w, jnp.bfloat16) for w in weights())
    wide = -(-PIECE // LANES) * LANES
    vmem = pl.BlockSpec(memory_space=pltpu.VMEM)
    return pl.pallas_call(
        body,
        out_shape=jax.ShapeDtypeStruct((PIECES, PIECE), jnp.bfloat16),
        in_specs=[vmem] * 7,
        out_specs=vmem,
        scratch_shapes=[
            pltpu.VMEM((ROWS, LANES), jnp.float32),
            pltpu.VMEM((2, PIECES, wide), jnp.float32),
        ],
        cost_estimate=pl.CostEstimate(flops=200_000_000, bytes_accessed=2_000_000, transcendentals=0),
        name="exchange",
    )(s0, s1, target, kernel_table(), left, fwd, inv)


def from_behind(block):
    count = lax.axis_size("blk")
    return lax.ppermute(block, "blk", [((i - 1) % count, i) for i in range(count)])


def shards(sources, targets):
    own = sources.reshape(PIECES, PIECE)
    target = from_behind(targets.reshape(PIECES, PIECE))
    behind = from_behind(own)
    partial = exchange_term(own, behind, target)
    arrived = lax.all_to_all(partial, "wide", split_axis=0, concat_axis=0, tiled=True)
    return arrived.astype(jnp.float32).sum(axis=0, keepdims=True)


def solution(mesh):
    in_specs = (P(("wide", "blk"), None), P("blk", None))
    return jax.shard_map(shards, mesh=mesh, in_specs=in_specs, out_specs=P("blk", "wide"), check_vma=False)
```

```python
import math

import jax
import jax.numpy as jnp
import numpy as np
from jax import lax
from jax.experimental import pallas as pl
from jax.experimental.pallas import tpu as pltpu
from jax.sharding import PartitionSpec as P

GRID = 40
ROWS = GRID * GRID
LANES = 128
HALF = 64
PIECES = 32
PIECE = GRID**3 // PIECES
GROUPS = PIECE // GRID
SCREEN = 0.3


def tables():
    index = np.arange(GRID)
    product = index[:, None] * index[None, :] % GRID
    folded = np.minimum(product, GRID - product)
    angle = 2.0 * math.pi / GRID * folded
    cos = np.cos(angle)
    sin = np.where(product <= GRID // 2, 1.0, -1.0) * np.sin(angle)
    sin = np.where((product == 0) | (product == GRID // 2), 0.0, sin)
    return cos.astype(np.float32), sin.astype(np.float32)


def weights():
    cos, sin = tables()

    def left(sign):
        return np.block([[cos, sign * sin], [-sign * sin, cos]])

    spread = np.zeros((2 * LANES, LANES), np.float32)
    first = np.zeros((LANES, 2 * LANES), np.float32)
    for row, col, table in ((0, 0, cos), (0, 1, -sin), (1, 0, sin), (1, 1, cos)):
        first[row * HALF : row * HALF + GRID, col * LANES : col * LANES + GRID] = table
    for row, col, table in ((0, 0, cos), (0, 1, sin), (1, 0, -sin), (1, 1, cos)):
        spread[row * LANES : row * LANES + GRID, col * HALF : col * HALF + GRID] = table
    return left(1.0), left(-1.0), first, spread


def kernel_table():
    index = jnp.arange(GRID, dtype=jnp.int32)
    wrapped = (index + GRID // 2) % GRID - GRID // 2
    wave = 2.0 * math.pi / GRID * wrapped.astype(jnp.float32)
    square = wave * wave
    lane = jnp.arange(LANES, dtype=jnp.int32) % GRID
    lane_wrapped = (lane + GRID // 2) % GRID - GRID // 2
    lane_wave = 2.0 * math.pi / GRID * lane_wrapped.astype(jnp.float32)
    lane_square = lane_wave * lane_wave
    total = square[None, :, None] + square[:, None, None] + lane_square[None, None, :]
    return 4.0 * math.pi / (total + SCREEN * SCREEN) / float(GRID**3)


def body(s0_ref, s1_ref, t_ref, kern_ref, fwd_ref, inv_ref, first_ref, last_ref, out_ref, xs, real, imag, flat, sums):
    lane = lax.broadcasted_iota(jnp.int32, (PIECES, LANES), 1)
    low = lane < HALF
    wide = flat.shape[2]

    target = t_ref[...]
    flat[0, :, :PIECE] = s0_ref[...] * target
    flat[1, :, :PIECE] = s1_ref[...] * target
    flat[:, :, PIECE:] = jnp.zeros((2, PIECES, wide - PIECE), jnp.bfloat16)

    def aligned(which, group, to):
        start = GRID * group
        tile, shift = start // LANES, start % LANES
        value = flat[which, :, tile * LANES : (tile + 1) * LANES]
        if shift + GRID > LANES:
            after = flat[which, :, (tile + 1) * LANES : (tile + 2) * LANES]
            value = jnp.where(lane >= shift, value, after)
        turn = (to - shift) % LANES
        return pltpu.roll(value, turn, 1) if turn else value

    for group in range(GROUPS):
        merged = jnp.where(low, aligned(0, group, 0), aligned(1, group, HALF))
        xs[pl.ds(group, PIECES, stride=GROUPS), :] = merged.astype(jnp.float32)

    forward, inverse = fwd_ref[...], inv_ref[...]
    re, im = slice(0, LANES), slice(LANES, 2 * LANES)

    def turned(table, first, second):
        both = jnp.concatenate([first, second], axis=1).astype(jnp.bfloat16)
        return jnp.dot(table, both, preferred_element_type=jnp.float32)

    def stacked(rows):
        return jnp.concatenate([real[rows, :], imag[rows, :]], axis=0)

    def put(rows, value):
        real[rows, :] = value[:GRID]
        imag[rows, :] = value[GRID:]

    def along_b(table):
        for pair in range(GRID // 2):
            one, two = pl.ds(2 * pair * GRID, GRID), pl.ds((2 * pair + 1) * GRID, GRID)
            value = turned(table, stacked(one), stacked(two))
            put(one, value[:, re])
            put(two, value[:, im])

    spread = jnp.dot(xs[...].astype(jnp.bfloat16), first_ref[...], preferred_element_type=jnp.float32)
    real[...] = spread[:, re]
    imag[...] = spread[:, im]
    along_b(forward)
    for pair in range(GRID // 2):
        one, two = pl.ds(2 * pair, GRID, stride=GRID), pl.ds(2 * pair + 1, GRID, stride=GRID)
        value = turned(forward, stacked(one), stacked(two))
        scale = [jnp.concatenate([kern_ref[2 * pair + which]] * 2, axis=0) for which in range(2)]
        value = turned(inverse, value[:, re] * scale[0], value[:, im] * scale[1])
        put(one, value[:, re])
        put(two, value[:, im])
    along_b(inverse)
    both = jnp.concatenate([real[...], imag[...]], axis=1).astype(jnp.bfloat16)
    xs[...] = jnp.dot(both, last_ref[...], preferred_element_type=jnp.float32)

    tiles = [[None] * (wide // LANES) for _ in range(2)]
    for group in range(GROUPS):
        start = GRID * group
        tile, shift = start // LANES, start % LANES
        value = xs[pl.ds(group, PIECES, stride=GROUPS), :].astype(jnp.bfloat16)
        for which in range(2):
            turn = (shift - HALF * which) % LANES
            moved = pltpu.roll(value, turn, 1) if turn else value
            held = tiles[which][tile]
            tiles[which][tile] = moved if held is None else jnp.where(lane >= shift, moved, held)
            if shift + GRID > LANES:
                tiles[which][tile + 1] = moved
    for tile in range(wide // LANES):
        size = min(LANES, PIECE - tile * LANES)
        here = slice(tile * LANES, tile * LANES + size)
        total = s0_ref[:, here].astype(jnp.float32) * tiles[0][tile][:, :size].astype(jnp.float32)
        total += s1_ref[:, here].astype(jnp.float32) * tiles[1][tile][:, :size].astype(jnp.float32)
        sums[pl.ds(tile, PIECES, stride=wide // LANES), :size] = -total
    out_ref[...] = sums[...].astype(jnp.bfloat16)


def exchange_term(s0, s1, target):
    tables_in = [jnp.asarray(w, jnp.bfloat16) for w in weights()]
    tiles = -(-PIECE // LANES)
    vmem = pl.BlockSpec(memory_space=pltpu.VMEM)
    return pl.pallas_call(
        body,
        out_shape=jax.ShapeDtypeStruct((PIECES * tiles, LANES), jnp.bfloat16),
        in_specs=[vmem] * 8,
        out_specs=vmem,
        scratch_shapes=[
            pltpu.VMEM((ROWS, LANES), jnp.float32),
            pltpu.VMEM((ROWS, LANES), jnp.float32),
            pltpu.VMEM((ROWS, LANES), jnp.float32),
            pltpu.VMEM((2, PIECES, tiles * LANES), jnp.bfloat16),
            pltpu.VMEM((PIECES * tiles, LANES), jnp.float32),
        ],
        compiler_params=pltpu.CompilerParams(vmem_limit_bytes=16 * 2**20),
        cost_estimate=pl.CostEstimate(flops=200_000_000, bytes_accessed=2_000_000, transcendentals=0),
        name="exchange",
    )(s0, s1, target, kernel_table(), *tables_in)


def from_behind(block):
    count = lax.axis_size("blk")
    return lax.ppermute(block, "blk", [((i - 1) % count, i) for i in range(count)])


def shards(sources, targets):
    own = sources.reshape(PIECES, PIECE)
    target = from_behind(targets.reshape(PIECES, PIECE))
    behind = from_behind(own)
    partial = exchange_term(own, behind, target)
    arrived = lax.all_to_all(partial, "wide", split_axis=0, concat_axis=0, tiled=True)
    summed = arrived.reshape(PIECES, -1, LANES).astype(jnp.float32).sum(axis=0)
    return summed.reshape(1, -1)[:, :PIECE]


def solution(mesh):
    in_specs = (P(("wide", "blk"), None), P("blk", None))
    return jax.shard_map(shards, mesh=mesh, in_specs=in_specs, out_specs=P("blk", "wide"), check_vma=False)
```

```python
import math

import jax
import jax.numpy as jnp
import numpy as np
from jax import lax
from jax.experimental import pallas as pl
from jax.experimental.pallas import tpu as pltpu
from jax.sharding import PartitionSpec as P

GRID = 40
ROWS = GRID * GRID
LANES = 128
HALF = 64
PIECES = 32
PIECE = GRID**3 // PIECES
GROUPS = PIECE // GRID
TILES = -(-PIECE // LANES)
WIDE = TILES * LANES
FLAT = GRID**3 // LANES
CYCLE = 8
BLOCK = 8
SCREEN = 0.3


def tables():
    index = np.arange(GRID)
    product = index[:, None] * index[None, :] % GRID
    folded = np.minimum(product, GRID - product)
    angle = 2.0 * math.pi / GRID * folded
    cos = np.cos(angle)
    sin = np.where(product <= GRID // 2, 1.0, -1.0) * np.sin(angle)
    sin = np.where((product == 0) | (product == GRID // 2), 0.0, sin)
    return cos.astype(np.float32), sin.astype(np.float32)


def weights():
    cos, sin = tables()

    def left(sign):
        return np.block([[cos, sign * sin], [-sign * sin, cos]])

    spread = np.zeros((2 * LANES, LANES), np.float32)
    first = np.zeros((LANES, 2 * LANES), np.float32)
    for row, col, table in ((0, 0, cos), (0, 1, -sin), (1, 0, sin), (1, 1, cos)):
        first[row * HALF : row * HALF + GRID, col * LANES : col * LANES + GRID] = table
    for row, col, table in ((0, 0, cos), (0, 1, sin), (1, 0, -sin), (1, 1, cos)):
        spread[row * LANES : row * LANES + GRID, col * HALF : col * HALF + GRID] = table
    return left(1.0), left(-1.0), first, spread


def kernel_table():
    index = jnp.arange(GRID, dtype=jnp.int32)
    wrapped = (index + GRID // 2) % GRID - GRID // 2
    wave = 2.0 * math.pi / GRID * wrapped.astype(jnp.float32)
    square = wave * wave
    lane = jnp.arange(LANES, dtype=jnp.int32) % GRID
    lane_wrapped = (lane + GRID // 2) % GRID - GRID // 2
    lane_wave = 2.0 * math.pi / GRID * lane_wrapped.astype(jnp.float32)
    lane_square = lane_wave * lane_wave
    total = square[None, :, None] + square[:, None, None] + lane_square[None, None, :]
    return 4.0 * math.pi / (total + SCREEN * SCREEN) / float(GRID**3)


def gather_body(s_ref, t_ref, out_ref, rows, pieces):
    lane = lax.broadcasted_iota(jnp.int32, (PIECES // CYCLE, LANES), 1)
    period = CYCLE * PIECE // LANES
    for which, ref in enumerate((s_ref, t_ref)):
        rows[:FLAT, :] = ref[...].astype(jnp.float32).reshape(FLAT, LANES)
        rows[FLAT:, :] = jnp.zeros((rows.shape[0] - FLAT, LANES), jnp.float32)
        for piece in range(CYCLE):
            for tile in range(TILES):
                row, shift = divmod(PIECE * piece + LANES * tile, LANES)
                value = rows[pl.ds(row, PIECES // CYCLE, stride=period), :]
                if shift:
                    after = rows[pl.ds(row + 1, PIECES // CYCLE, stride=period), :]
                    value = pltpu.roll(jnp.where(lane >= shift, value, after), LANES - shift, 1)
                start = which * PIECES + piece
                pieces[tile, pl.ds(start, PIECES // CYCLE, stride=CYCLE), :] = value
    for tile in range(TILES):
        out_ref[:, tile * LANES : (tile + 1) * LANES] = pieces[tile].astype(jnp.bfloat16)


def body(own_ref, came_ref, kern_ref, fwd_ref, inv_ref, first_ref, last_ref, out_ref, xs, real, imag, flat, sums):
    lane = lax.broadcasted_iota(jnp.int32, (PIECES, LANES), 1)
    low = lane < HALF

    target = came_ref[PIECES:, :]
    flat[0] = own_ref[:PIECES, :] * target
    flat[1] = came_ref[:PIECES, :] * target

    def aligned(which, group, to):
        start = GRID * group
        tile, shift = start // LANES, start % LANES
        value = flat[which, :, tile * LANES : (tile + 1) * LANES]
        if shift + GRID > LANES:
            after = flat[which, :, (tile + 1) * LANES : (tile + 2) * LANES]
            value = jnp.where(lane >= shift, value, after)
        turn = (to - shift) % LANES
        return pltpu.roll(value, turn, 1) if turn else value

    for group in range(GROUPS):
        merged = jnp.where(low, aligned(0, group, 0), aligned(1, group, HALF))
        xs[pl.ds(group, PIECES, stride=GROUPS), :] = merged.astype(jnp.float32)

    forward, inverse = fwd_ref[...], inv_ref[...]
    re, im = slice(0, LANES), slice(LANES, 2 * LANES)

    def turned(table, first, second):
        both = jnp.concatenate([first, second], axis=1).astype(jnp.bfloat16)
        return jnp.dot(table, both, preferred_element_type=jnp.float32)

    def stacked(rows):
        return jnp.concatenate([real[rows, :], imag[rows, :]], axis=0)

    def put(rows, value):
        real[rows, :] = value[:GRID]
        imag[rows, :] = value[GRID:]

    def along_b(table):
        for pair in range(GRID // 2):
            one, two = pl.ds(2 * pair * GRID, GRID), pl.ds((2 * pair + 1) * GRID, GRID)
            value = turned(table, stacked(one), stacked(two))
            put(one, value[:, re])
            put(two, value[:, im])

    spread = jnp.dot(xs[...].astype(jnp.bfloat16), first_ref[...], preferred_element_type=jnp.float32)
    real[...] = spread[:, re]
    imag[...] = spread[:, im]
    along_b(forward)
    for pair in range(GRID // 2):
        one, two = pl.ds(2 * pair, GRID, stride=GRID), pl.ds(2 * pair + 1, GRID, stride=GRID)
        value = turned(forward, stacked(one), stacked(two))
        scale = [jnp.concatenate([kern_ref[2 * pair + which]] * 2, axis=0) for which in range(2)]
        value = turned(inverse, value[:, re] * scale[0], value[:, im] * scale[1])
        put(one, value[:, re])
        put(two, value[:, im])
    along_b(inverse)
    both = jnp.concatenate([real[...], imag[...]], axis=1).astype(jnp.bfloat16)
    xs[...] = jnp.dot(both, last_ref[...], preferred_element_type=jnp.float32)

    tiles = [[None] * TILES for _ in range(2)]
    for group in range(GROUPS):
        start = GRID * group
        tile, shift = start // LANES, start % LANES
        value = xs[pl.ds(group, PIECES, stride=GROUPS), :].astype(jnp.bfloat16)
        for which in range(2):
            turn = (shift - HALF * which) % LANES
            moved = pltpu.roll(value, turn, 1) if turn else value
            held = tiles[which][tile]
            tiles[which][tile] = moved if held is None else jnp.where(lane >= shift, moved, held)
            if shift + GRID > LANES:
                tiles[which][tile + 1] = moved
    for tile in range(TILES):
        here = slice(tile * LANES, (tile + 1) * LANES)
        total = own_ref[:PIECES, here].astype(jnp.float32) * tiles[0][tile].astype(jnp.float32)
        total += came_ref[:PIECES, here].astype(jnp.float32) * tiles[1][tile].astype(jnp.float32)
        sums[pl.ds(tile, PIECES, stride=TILES), :] = -total
    out_ref[...] = sums[...].astype(jnp.bfloat16)


VMEM = pl.BlockSpec(memory_space=pltpu.VMEM)
PARAMS = pltpu.CompilerParams(vmem_limit_bytes=16 * 2**20)


def gathered(sources, targets):
    return pl.pallas_call(
        gather_body,
        out_shape=jax.ShapeDtypeStruct((2 * PIECES, WIDE), jnp.bfloat16),
        in_specs=[VMEM] * 2,
        out_specs=VMEM,
        scratch_shapes=[
            pltpu.VMEM((FLAT + 4, LANES), jnp.float32),
            pltpu.VMEM((TILES, 2 * PIECES, LANES), jnp.float32),
        ],
        compiler_params=PARAMS,
        cost_estimate=pl.CostEstimate(flops=1_000_000, bytes_accessed=800_000, transcendentals=0),
        name="gather",
    )(sources, targets)


def exchange_term(own, came):
    constants = [jnp.asarray(w, jnp.bfloat16) for w in weights()]
    return pl.pallas_call(
        body,
        out_shape=jax.ShapeDtypeStruct((PIECES * TILES, LANES), jnp.bfloat16),
        in_specs=[VMEM] * 7,
        out_specs=VMEM,
        scratch_shapes=[
            pltpu.VMEM((ROWS, LANES), jnp.float32),
            pltpu.VMEM((ROWS, LANES), jnp.float32),
            pltpu.VMEM((ROWS, LANES), jnp.float32),
            pltpu.VMEM((2, PIECES, WIDE), jnp.bfloat16),
            pltpu.VMEM((PIECES * TILES, LANES), jnp.float32),
        ],
        compiler_params=PARAMS,
        cost_estimate=pl.CostEstimate(flops=200_000_000, bytes_accessed=2_000_000, transcendentals=0),
        name="exchange",
    )(own, came, kernel_table(), *constants)


def from_behind(block):
    wide, blk = lax.axis_size("wide"), lax.axis_size("blk")

    def source(w, b):
        return w * blk + b - 1 if b else (w - BLOCK) % wide * blk + blk - 1

    route = [(source(w, b), w * blk + b) for w in range(wide) for b in range(blk)]
    return lax.ppermute(block, ("wide", "blk"), route)


def shards(sources, targets):
    own = gathered(sources, targets)
    partial = exchange_term(own, from_behind(own))
    arrived = lax.all_to_all(partial, "wide", split_axis=0, concat_axis=0, tiled=True)
    summed = arrived.reshape(PIECES, -1, LANES).astype(jnp.float32).sum(axis=0)
    return summed.reshape(1, -1)[:, :PIECE]


def solution(mesh):
    in_specs = (P(("wide", "blk"), None), P("blk", None))
    return jax.shard_map(shards, mesh=mesh, in_specs=in_specs, out_specs=P("blk", "wide"), check_vma=False)
```

```python
import math

import jax
import jax.numpy as jnp
import numpy as np
from jax import lax
from jax.experimental import pallas as pl
from jax.experimental.pallas import tpu as pltpu
from jax.sharding import PartitionSpec as P


GRID = 40
ROWS = GRID * GRID
LANES = 128
HALF = 64
PIECES = 32
PIECE = GRID**3 // PIECES
GROUPS = PIECE // GRID
TILES = -(-PIECE // LANES)
WIDE = TILES * LANES
FLAT = GRID**3 // LANES
CYCLE = 8
PARTS = 4
ROUNDS = ({2: 0}, {3: 0}, {0: 3, 1: 0, 3: 1}, {0: 1}, {0: 2, 1: 3, 2: 1}, {3: 2}, {1: 2, 2: 3})
BLOCK = 8
SCREEN = 0.3


def tables():
    index = np.arange(GRID)
    product = index[:, None] * index[None, :] % GRID
    folded = np.minimum(product, GRID - product)
    angle = 2.0 * math.pi / GRID * folded
    cos = np.cos(angle)
    sin = np.where(product <= GRID // 2, 1.0, -1.0) * np.sin(angle)
    sin = np.where((product == 0) | (product == GRID // 2), 0.0, sin)
    return cos.astype(np.float32), sin.astype(np.float32)


def weights():
    cos, sin = tables()

    def left(sign):
        return np.block([[cos, sign * sin], [-sign * sin, cos]])

    spread = np.zeros((2 * LANES, LANES), np.float32)
    first = np.zeros((LANES, 2 * LANES), np.float32)
    for row, col, table in ((0, 0, cos), (0, 1, -sin), (1, 0, sin), (1, 1, cos)):
        first[row * HALF : row * HALF + GRID, col * LANES : col * LANES + GRID] = table
    for row, col, table in ((0, 0, cos), (0, 1, sin), (1, 0, -sin), (1, 1, cos)):
        spread[row * LANES : row * LANES + GRID, col * HALF : col * HALF + GRID] = table
    return left(1.0), left(-1.0), first, spread


def kernel_table():
    index = jnp.arange(GRID, dtype=jnp.int32)
    wrapped = (index + GRID // 2) % GRID - GRID // 2
    wave = 2.0 * math.pi / GRID * wrapped.astype(jnp.float32)
    square = wave * wave
    lane = jnp.arange(LANES, dtype=jnp.int32) % GRID
    lane_wrapped = (lane + GRID // 2) % GRID - GRID // 2
    lane_wave = 2.0 * math.pi / GRID * lane_wrapped.astype(jnp.float32)
    lane_square = lane_wave * lane_wave
    total = square[None, :, None] + square[:, None, None] + lane_square[None, None, :]
    return 4.0 * math.pi / (total + SCREEN * SCREEN) / float(GRID**3)


def gather_body(s_ref, t_ref, out_ref, raw, rows, pieces, ready, arrived, left):
    copies = []
    for which, ref in enumerate((s_ref, t_ref)):
        for part in range(PARTS):
            here = pl.ds(part * GRID**3 // PARTS, GRID**3 // PARTS)
            copies.append(pltpu.make_async_copy(ref.at[:, here], raw.at[which, :, here], arrived.at[which, part]))
    for copy in copies:
        copy.start()
    lane = lax.broadcasted_iota(jnp.int32, (PIECES // CYCLE, LANES), 1)
    period = CYCLE * PIECE // LANES
    for which in range(2):
        for copy in copies[which * PARTS : (which + 1) * PARTS]:
            copy.wait()
        rows[:FLAT, :] = raw[which].astype(jnp.float32).reshape(FLAT, LANES)
        rows[FLAT:, :] = jnp.zeros((rows.shape[0] - FLAT, LANES), jnp.float32)
        for piece in range(CYCLE):
            for tile in range(TILES):
                row, shift = divmod(PIECE * piece + LANES * tile, LANES)
                value = rows[pl.ds(row, PIECES // CYCLE, stride=period), :]
                if shift:
                    after = rows[pl.ds(row + 1, PIECES // CYCLE, stride=period), :]
                    value = pltpu.roll(jnp.where(lane >= shift, value, after), LANES - shift, 1)
                pieces[which, tile, pl.ds(piece, PIECES // CYCLE, stride=CYCLE), :] = value
        for tile in range(TILES):
            ready[which, :, tile * LANES : (tile + 1) * LANES] = pieces[which, tile].astype(jnp.bfloat16)
        copies.append(pltpu.make_async_copy(ready.at[which], out_ref.at[pl.ds(which * PIECES, PIECES)], left.at[which]))
        copies[-1].start()
    for copy in copies[-2:]:
        copy.wait()


def body(own_ref, came_ref, kern_ref, fwd_ref, inv_ref, first_ref, last_ref, out_ref, xs, real, imag, flat, sums):
    lane = lax.broadcasted_iota(jnp.int32, (PIECES, LANES), 1)
    low = lane < HALF

    target = came_ref[PIECES:, :]
    flat[0] = own_ref[:PIECES, :] * target
    flat[1] = came_ref[:PIECES, :] * target

    def aligned(which, group, to):
        start = GRID * group
        tile, shift = start // LANES, start % LANES
        value = flat[which, :, tile * LANES : (tile + 1) * LANES]
        if shift + GRID > LANES:
            after = flat[which, :, (tile + 1) * LANES : (tile + 2) * LANES]
            value = jnp.where(lane >= shift, value, after)
        turn = (to - shift) % LANES
        return pltpu.roll(value, turn, 1) if turn else value

    for group in range(GROUPS):
        merged = jnp.where(low, aligned(0, group, 0), aligned(1, group, HALF))
        xs[pl.ds(group, PIECES, stride=GROUPS), :] = merged.astype(jnp.float32)

    forward, inverse = fwd_ref[...], inv_ref[...]
    re, im = slice(0, LANES), slice(LANES, 2 * LANES)

    def turned(table, first, second):
        both = jnp.concatenate([first, second], axis=1).astype(jnp.bfloat16)
        return jnp.dot(table, both, preferred_element_type=jnp.float32)

    def stacked(rows):
        return jnp.concatenate([real[rows, :], imag[rows, :]], axis=0)

    def put(rows, value):
        real[rows, :] = value[:GRID]
        imag[rows, :] = value[GRID:]

    def along_b(table):
        for pair in range(GRID // 2):
            one, two = pl.ds(2 * pair * GRID, GRID), pl.ds((2 * pair + 1) * GRID, GRID)
            value = turned(table, stacked(one), stacked(two))
            put(one, value[:, re])
            put(two, value[:, im])

    spread = jnp.dot(xs[...].astype(jnp.bfloat16), first_ref[...], preferred_element_type=jnp.float32)
    real[...] = spread[:, re]
    imag[...] = spread[:, im]
    along_b(forward)
    for pair in range(GRID // 2):
        one, two = pl.ds(2 * pair, GRID, stride=GRID), pl.ds(2 * pair + 1, GRID, stride=GRID)
        value = turned(forward, stacked(one), stacked(two))
        scale = [jnp.concatenate([kern_ref[2 * pair + which]] * 2, axis=0) for which in range(2)]
        value = turned(inverse, value[:, re] * scale[0], value[:, im] * scale[1])
        put(one, value[:, re])
        put(two, value[:, im])
    along_b(inverse)
    both = jnp.concatenate([real[...], imag[...]], axis=1).astype(jnp.bfloat16)
    xs[...] = jnp.dot(both, last_ref[...], preferred_element_type=jnp.float32)

    tiles = [[None] * TILES for _ in range(2)]
    for group in range(GROUPS):
        start = GRID * group
        tile, shift = start // LANES, start % LANES
        value = xs[pl.ds(group, PIECES, stride=GROUPS), :].astype(jnp.bfloat16)
        for which in range(2):
            turn = (shift - HALF * which) % LANES
            moved = pltpu.roll(value, turn, 1) if turn else value
            held = tiles[which][tile]
            tiles[which][tile] = moved if held is None else jnp.where(lane >= shift, moved, held)
            if shift + GRID > LANES:
                tiles[which][tile + 1] = moved
    for tile in range(TILES):
        here = slice(tile * LANES, (tile + 1) * LANES)
        total = own_ref[:PIECES, here].astype(jnp.float32) * tiles[0][tile].astype(jnp.float32)
        total += came_ref[:PIECES, here].astype(jnp.float32) * tiles[1][tile].astype(jnp.float32)
        for part in range(PARTS):
            sums[pl.ds(part * TILES + tile, BLOCK, stride=PARTS * TILES), :] = -total[part * BLOCK : (part + 1) * BLOCK]
    out_ref[...] = sums[...].astype(jnp.bfloat16)


VMEM = pl.BlockSpec(memory_space=pltpu.VMEM)
PARAMS = pltpu.CompilerParams(vmem_limit_bytes=16 * 2**20)


def gathered(sources, targets):
    return pl.pallas_call(
        gather_body,
        out_shape=jax.ShapeDtypeStruct((2 * PIECES, WIDE), jnp.bfloat16),
        in_specs=[pl.BlockSpec(memory_space=pltpu.HBM)] * 2,
        out_specs=pl.BlockSpec(memory_space=pltpu.HBM),
        scratch_shapes=[
            pltpu.VMEM((2, 1, GRID**3), jnp.bfloat16),
            pltpu.VMEM((FLAT + 4, LANES), jnp.float32),
            pltpu.VMEM((2, TILES, PIECES, LANES), jnp.float32),
            pltpu.VMEM((2, PIECES, WIDE), jnp.bfloat16),
            pltpu.SemaphoreType.DMA((2, PARTS)),
            pltpu.SemaphoreType.DMA((2,)),
        ],
        compiler_params=pltpu.CompilerParams(vmem_limit_bytes=61000 * 1024),
        cost_estimate=pl.CostEstimate(flops=1_000_000, bytes_accessed=800_000, transcendentals=0),
        name="gather",
    )(sources, targets)


def exchange_term(own, came):
    constants = [jnp.asarray(w, jnp.bfloat16) for w in weights()]
    return pl.pallas_call(
        body,
        out_shape=jax.ShapeDtypeStruct((PIECES * TILES, LANES), jnp.bfloat16),
        in_specs=[VMEM] * 7,
        out_specs=VMEM,
        scratch_shapes=[
            pltpu.VMEM((ROWS, LANES), jnp.float32),
            pltpu.VMEM((ROWS, LANES), jnp.float32),
            pltpu.VMEM((ROWS, LANES), jnp.float32),
            pltpu.VMEM((2, PIECES, WIDE), jnp.bfloat16),
            pltpu.VMEM((PIECES * TILES, LANES), jnp.float32),
        ],
        compiler_params=PARAMS,
        cost_estimate=pl.CostEstimate(flops=200_000_000, bytes_accessed=2_000_000, transcendentals=0),
        name="exchange",
    )(own, came, kernel_table(), *constants)


def from_behind(block):
    count = lax.axis_size("blk")
    return lax.ppermute(block, "blk", [((i - 1) % count, i) for i in range(count)])


def block_sum_body(came_ref, own_ref, *refs):
    *out_refs, held = refs
    total = came_ref[0].astype(jnp.float32)
    for other in range(1, BLOCK):
        total += came_ref[other].astype(jnp.float32)
    held[...] = total
    part = lax.div(lax.axis_index("wide"), BLOCK)
    own_ref[...] = held[pl.ds(pl.multiple_of(part * TILES, TILES), TILES), :]
    for ends, out_ref in zip(ROUNDS, out_refs, strict=True):
        end = jnp.int32(0)
        for start, chosen in ends.items():
            end = jnp.where(part == start, chosen, end)
        out_ref[...] = held[pl.ds(pl.multiple_of(end * TILES, TILES), TILES), :].astype(jnp.bfloat16)


def block_sum(came):
    shape = (TILES, LANES)
    return pl.pallas_call(
        block_sum_body,
        out_shape=[jax.ShapeDtypeStruct(shape, jnp.float32)] + [jax.ShapeDtypeStruct(shape, jnp.bfloat16)] * len(ROUNDS),
        in_specs=[VMEM],
        out_specs=[VMEM] * (1 + len(ROUNDS)),
        scratch_shapes=[pltpu.VMEM((PARTS * TILES, LANES), jnp.float32)],
        compiler_params=PARAMS,
        cost_estimate=pl.CostEstimate(flops=100_000, bytes_accessed=150_000, transcendentals=0),
        name="block_sum",
    )(came)


def last_sum_body(own_ref, *refs):
    total = own_ref[...]
    for ref in refs[:-1]:
        total += ref[...].astype(jnp.float32)
    refs[-1][...] = total


def last_sum(own, came):
    return pl.pallas_call(
        last_sum_body,
        out_shape=jax.ShapeDtypeStruct((TILES, LANES), jnp.float32),
        in_specs=[VMEM] * (1 + len(came)),
        out_specs=VMEM,
        compiler_params=PARAMS,
        cost_estimate=pl.CostEstimate(flops=100_000, bytes_accessed=80_000, transcendentals=0),
        name="last_sum",
    )(own, *came)


def shards(sources, targets):
    own = gathered(sources, targets)
    partial = exchange_term(own, from_behind(own))
    groups = [[part * BLOCK + i for i in range(BLOCK)] for part in range(PARTS)]
    came = lax.all_to_all(partial, "wide", split_axis=0, concat_axis=0, axis_index_groups=groups, tiled=True)
    mine, *sent = block_sum(came.reshape(BLOCK, PARTS * TILES, LANES))
    arrived = []
    for turn, ends in enumerate(ROUNDS):
        route = [(start * BLOCK + i, end * BLOCK + i) for start, end in ends.items() for i in range(BLOCK)]
        arrived.append(lax.ppermute(sent[turn], "wide", route))
    return last_sum(mine, arrived).reshape(1, -1)[:, :PIECE]


def solution(mesh):
    in_specs = (P(("wide", "blk"), None), P("blk", None))
    return jax.shard_map(shards, mesh=mesh, in_specs=in_specs, out_specs=P("blk", "wide"), check_vma=False)
```

```python
import math

import jax
import jax.numpy as jnp
import numpy as np
from jax import lax
from jax.experimental import pallas as pl
from jax.experimental.pallas import tpu as pltpu
from jax.sharding import PartitionSpec as P


GRID = 40
ROWS = GRID * GRID
LANES = 128
HALF = 64
PIECES = 32
PIECE = GRID**3 // PIECES
GROUPS = PIECE // GRID
TILES = -(-PIECE // LANES)
WIDE = TILES * LANES
FLAT = GRID**3 // LANES
CYCLE = 8
PARTS = 4
STEPS = 2
ROUNDS = ({2: 0}, {3: 0}, {0: 3, 1: 0, 3: 1}, {0: 1}, {0: 2, 1: 3, 2: 1}, {3: 2}, {1: 2, 2: 3})
BLOCK = 8
SCREEN = 0.3


def tables():
    index = np.arange(GRID)
    product = index[:, None] * index[None, :] % GRID
    folded = np.minimum(product, GRID - product)
    angle = 2.0 * math.pi / GRID * folded
    cos = np.cos(angle)
    sin = np.where(product <= GRID // 2, 1.0, -1.0) * np.sin(angle)
    sin = np.where((product == 0) | (product == GRID // 2), 0.0, sin)
    return cos.astype(np.float32), sin.astype(np.float32)


def weights():
    cos, sin = tables()

    def left(sign):
        return np.block([[cos, sign * sin], [-sign * sin, cos]])

    first = np.zeros((2 * LANES, 2 * LANES), np.float32)
    spread = np.zeros((2 * LANES, 2 * LANES), np.float32)
    for plane in range(2):
        for row, col, cosine, sine in ((0, 0, cos, 0.0), (0, 1, 0.0, -sin), (1, 0, 0.0, sin), (1, 1, cos, 0.0)):
            near, far = plane * LANES + row * HALF, col * LANES + plane * HALF
            first[near : near + GRID, far : far + GRID] = cosine + sine
        for row, col, cosine, sine in ((0, 0, cos, 0.0), (0, 1, 0.0, sin), (1, 0, 0.0, -sin), (1, 1, cos, 0.0)):
            near, far = row * LANES + plane * HALF, plane * LANES + col * HALF
            spread[near : near + GRID, far : far + GRID] = cosine + sine
    return left(1.0), left(-1.0), first, spread


def kernel_table():
    index = jnp.arange(GRID, dtype=jnp.int32)
    wrapped = (index + GRID // 2) % GRID - GRID // 2
    wave = 2.0 * math.pi / GRID * wrapped.astype(jnp.float32)
    square = wave * wave
    lane = jnp.arange(LANES, dtype=jnp.int32) % GRID
    lane_wrapped = (lane + GRID // 2) % GRID - GRID // 2
    lane_wave = 2.0 * math.pi / GRID * lane_wrapped.astype(jnp.float32)
    lane_square = lane_wave * lane_wave
    total = square[None, :, None] + square[:, None, None] + lane_square[None, None, :]
    return 4.0 * math.pi / (total + SCREEN * SCREEN) / float(GRID**3)


def gather_body(s_ref, t_ref, out_ref, raw, rows, pieces, ready, arrived, left):
    copies = []
    for which, ref in enumerate((s_ref, t_ref)):
        for part in range(PARTS):
            here = pl.ds(part * GRID**3 // PARTS, GRID**3 // PARTS)
            copies.append(pltpu.make_async_copy(ref.at[:, here], raw.at[which, :, here], arrived.at[which, part]))
    for copy in copies:
        copy.start()
    lane = lax.broadcasted_iota(jnp.int32, (PIECES // CYCLE, LANES), 1)
    period = CYCLE * PIECE // LANES
    for which in range(2):
        for copy in copies[which * PARTS : (which + 1) * PARTS]:
            copy.wait()
        rows[:FLAT, :] = raw[which].astype(jnp.float32).reshape(FLAT, LANES)
        rows[FLAT:, :] = jnp.zeros((rows.shape[0] - FLAT, LANES), jnp.float32)
        for piece in range(CYCLE):
            for tile in range(TILES):
                row, shift = divmod(PIECE * piece + LANES * tile, LANES)
                value = rows[pl.ds(row, PIECES // CYCLE, stride=period), :]
                if shift:
                    after = rows[pl.ds(row + 1, PIECES // CYCLE, stride=period), :]
                    value = pltpu.roll(jnp.where(lane >= shift, value, after), LANES - shift, 1)
                pieces[which, tile, pl.ds(piece, PIECES // CYCLE, stride=CYCLE), :] = value
        for tile in range(TILES):
            ready[which, :, tile * LANES : (tile + 1) * LANES] = pieces[which, tile].astype(jnp.bfloat16)
        copies.append(pltpu.make_async_copy(ready.at[which], out_ref.at[pl.ds(which * PIECES, PIECES)], left.at[which]))
        copies[-1].start()
    for copy in copies[-2:]:
        copy.wait()


def body(own_ref, came_ref, kern_ref, fwd_ref, inv_ref, first_ref, last_ref, out_ref, xs, near, real, imag, real_back, imag_back, back, ys, flat, sums):
    lane = lax.broadcasted_iota(jnp.int32, (PIECES, LANES), 1)
    low = lane < HALF

    target = came_ref[PIECES:, :]
    flat[0] = own_ref[:PIECES, :] * target
    flat[1] = came_ref[:PIECES, :] * target

    def aligned(which, group, to):
        start = GRID * group
        tile, shift = start // LANES, start % LANES
        value = flat[which, :, tile * LANES : (tile + 1) * LANES]
        if shift + GRID > LANES:
            after = flat[which, :, (tile + 1) * LANES : (tile + 2) * LANES]
            value = jnp.where(lane >= shift, value, after)
        turn = (to - shift) % LANES
        return pltpu.roll(value, turn, 1) if turn else value

    for group in range(GROUPS):
        merged = jnp.where(low, aligned(0, group, 0), aligned(1, group, HALF))
        xs[pl.ds(group, PIECES, stride=GROUPS), :] = merged.astype(jnp.float32)

    forward, inverse = fwd_ref[...], inv_ref[...]
    re, im = slice(0, LANES), slice(LANES, 2 * LANES)

    def turned(table, first, second):
        both = jnp.concatenate([first, second], axis=1).astype(jnp.bfloat16)
        return jnp.dot(table, both, preferred_element_type=jnp.float32)

    def stacked(rows):
        return jnp.concatenate([real[rows, :], imag[rows, :]], axis=0)

    def put(refs, rows, value):
        refs[0][rows, :] = value[:GRID]
        refs[1][rows, :] = value[GRID:]

    def plane(index):
        return pl.ds(index * GRID, GRID)

    def paired(index):
        rows, far = plane(index), plane(index + GRID // 2)
        both = [jnp.where(low_rows, ref[rows, :], pltpu.roll(ref[far, :], HALF, 1)) for ref in (real_back, imag_back)]
        return jnp.concatenate(both, axis=0)

    low_rows = lax.broadcasted_iota(jnp.int32, (GRID, LANES), 1) < HALF

    def along_c(source, table_ref, result, step):
        size = ROWS // 2 // STEPS
        one, two = pl.ds(step * size, size), pl.ds(ROWS // 2 + step * size, size)
        both = jnp.concatenate([source[one, :], source[two, :]], axis=1).astype(jnp.bfloat16)
        value = jnp.dot(both, table_ref[...], preferred_element_type=jnp.float32)
        result[one, :] = value[:, re]
        result[two, :] = value[:, im]

    pairs = GRID // 4 // STEPS
    for step in range(STEPS):
        along_c(xs, first_ref, near, step)
    for step in range(STEPS):
        for pair in range(step * pairs, (step + 1) * pairs):
            chosen = (2 * pair, 2 * pair + 1)
            slabs = [jnp.concatenate([near[plane(index), :], near[plane(index + GRID // 2), :]], axis=0) for index in chosen]
            value = turned(forward, *slabs)
            for index, part in zip(chosen, (re, im), strict=True):
                put((real, imag), plane(index), value[:, part])
                put((real, imag), plane(index + GRID // 2), pltpu.roll(value[:, part], HALF, 1))
    for pair in range(GRID // 2):
        one, two = pl.ds(2 * pair, GRID, stride=GRID), pl.ds(2 * pair + 1, GRID, stride=GRID)
        value = turned(forward, stacked(one), stacked(two))
        scale = [jnp.concatenate([kern_ref[2 * pair + which]] * 2, axis=0) for which in range(2)]
        value = turned(inverse, value[:, re] * scale[0], value[:, im] * scale[1])
        put((real_back, imag_back), one, value[:, re])
        put((real_back, imag_back), two, value[:, im])
    for step in range(STEPS):
        for pair in range(step * pairs, (step + 1) * pairs):
            value = turned(inverse, paired(2 * pair), paired(2 * pair + 1))
            for index, part in ((2 * pair, re), (2 * pair + 1, im)):
                back[plane(index), :] = value[:GRID, part]
                back[plane(index + GRID // 2), :] = value[GRID:, part]
    for step in range(STEPS):
        along_c(back, last_ref, ys, step)

    tiles = [[None] * TILES for _ in range(2)]
    for group in range(GROUPS):
        start = GRID * group
        tile, shift = start // LANES, start % LANES
        value = ys[pl.ds(group, PIECES, stride=GROUPS), :].astype(jnp.bfloat16)
        for which in range(2):
            turn = (shift - HALF * which) % LANES
            moved = pltpu.roll(value, turn, 1) if turn else value
            held = tiles[which][tile]
            tiles[which][tile] = moved if held is None else jnp.where(lane >= shift, moved, held)
            if shift + GRID > LANES:
                tiles[which][tile + 1] = moved
    for tile in range(TILES):
        here = slice(tile * LANES, (tile + 1) * LANES)
        total = own_ref[:PIECES, here].astype(jnp.float32) * tiles[0][tile].astype(jnp.float32)
        total += came_ref[:PIECES, here].astype(jnp.float32) * tiles[1][tile].astype(jnp.float32)
        for part in range(PARTS):
            sums[pl.ds(part * TILES + tile, BLOCK, stride=PARTS * TILES), :] = -total[part * BLOCK : (part + 1) * BLOCK]
    out_ref[...] = sums[...].astype(jnp.bfloat16)


VMEM = pl.BlockSpec(memory_space=pltpu.VMEM)
PARAMS = pltpu.CompilerParams(vmem_limit_bytes=16 * 2**20)


def gathered(sources, targets):
    return pl.pallas_call(
        gather_body,
        out_shape=jax.ShapeDtypeStruct((2 * PIECES, WIDE), jnp.bfloat16),
        in_specs=[pl.BlockSpec(memory_space=pltpu.HBM)] * 2,
        out_specs=pl.BlockSpec(memory_space=pltpu.HBM),
        scratch_shapes=[
            pltpu.VMEM((2, 1, GRID**3), jnp.bfloat16),
            pltpu.VMEM((FLAT + 4, LANES), jnp.float32),
            pltpu.VMEM((2, TILES, PIECES, LANES), jnp.float32),
            pltpu.VMEM((2, PIECES, WIDE), jnp.bfloat16),
            pltpu.SemaphoreType.DMA((2, PARTS)),
            pltpu.SemaphoreType.DMA((2,)),
        ],
        compiler_params=pltpu.CompilerParams(vmem_limit_bytes=61000 * 1024),
        cost_estimate=pl.CostEstimate(flops=1_000_000, bytes_accessed=800_000, transcendentals=0),
        name="gather",
    )(sources, targets)


def exchange_term(own, came):
    constants = [jnp.asarray(w, jnp.bfloat16) for w in weights()]
    return pl.pallas_call(
        body,
        out_shape=jax.ShapeDtypeStruct((PIECES * TILES, LANES), jnp.bfloat16),
        in_specs=[VMEM] * 7,
        out_specs=VMEM,
        scratch_shapes=[
            *[pltpu.VMEM((ROWS, LANES), jnp.float32)] * 8,
            pltpu.VMEM((2, PIECES, WIDE), jnp.bfloat16),
            pltpu.VMEM((PIECES * TILES, LANES), jnp.float32),
        ],
        compiler_params=PARAMS,
        cost_estimate=pl.CostEstimate(flops=200_000_000, bytes_accessed=2_000_000, transcendentals=0),
        name="exchange",
    )(own, came, kernel_table(), *constants)


def from_behind(block):
    count = lax.axis_size("blk")
    return lax.ppermute(block, "blk", [((i - 1) % count, i) for i in range(count)])


def block_sum_body(came_ref, own_ref, *refs):
    *out_refs, held = refs
    total = came_ref[0].astype(jnp.float32)
    for other in range(1, BLOCK):
        total += came_ref[other].astype(jnp.float32)
    held[...] = total
    part = lax.div(lax.axis_index("wide"), BLOCK)
    own_ref[...] = held[pl.ds(pl.multiple_of(part * TILES, TILES), TILES), :]
    for ends, out_ref in zip(ROUNDS, out_refs, strict=True):
        end = jnp.int32(0)
        for start, chosen in ends.items():
            end = jnp.where(part == start, chosen, end)
        out_ref[...] = held[pl.ds(pl.multiple_of(end * TILES, TILES), TILES), :].astype(jnp.bfloat16)


def block_sum(came):
    shape = (TILES, LANES)
    return pl.pallas_call(
        block_sum_body,
        out_shape=[jax.ShapeDtypeStruct(shape, jnp.float32)] + [jax.ShapeDtypeStruct(shape, jnp.bfloat16)] * len(ROUNDS),
        in_specs=[VMEM],
        out_specs=[VMEM] * (1 + len(ROUNDS)),
        scratch_shapes=[pltpu.VMEM((PARTS * TILES, LANES), jnp.float32)],
        compiler_params=PARAMS,
        cost_estimate=pl.CostEstimate(flops=100_000, bytes_accessed=150_000, transcendentals=0),
        name="block_sum",
    )(came)


def last_sum_body(own_ref, *refs):
    total = own_ref[...]
    for ref in refs[:-1]:
        total += ref[...].astype(jnp.float32)
    refs[-1][...] = total


def last_sum(own, came):
    return pl.pallas_call(
        last_sum_body,
        out_shape=jax.ShapeDtypeStruct((TILES, LANES), jnp.float32),
        in_specs=[VMEM] * (1 + len(came)),
        out_specs=VMEM,
        compiler_params=PARAMS,
        cost_estimate=pl.CostEstimate(flops=100_000, bytes_accessed=80_000, transcendentals=0),
        name="last_sum",
    )(own, *came)


def shards(sources, targets):
    own = gathered(sources, targets)
    partial = exchange_term(own, from_behind(own))
    groups = [[part * BLOCK + i for i in range(BLOCK)] for part in range(PARTS)]
    came = lax.all_to_all(partial, "wide", split_axis=0, concat_axis=0, axis_index_groups=groups, tiled=True)
    mine, *sent = block_sum(came.reshape(BLOCK, PARTS * TILES, LANES))
    arrived = []
    for turn, ends in enumerate(ROUNDS):
        route = [(start * BLOCK + i, end * BLOCK + i) for start, end in ends.items() for i in range(BLOCK)]
        arrived.append(lax.ppermute(sent[turn], "wide", route))
    return last_sum(mine, arrived).reshape(1, -1)[:, :PIECE]


def solution(mesh):
    in_specs = (P(("wide", "blk"), None), P("blk", None))
    return jax.shard_map(shards, mesh=mesh, in_specs=in_specs, out_specs=P("blk", "wide"), check_vma=False)
```

```python
import math

import jax
import jax.numpy as jnp
import numpy as np
from jax import lax
from jax.experimental import pallas as pl
from jax.experimental.pallas import tpu as pltpu
from jax.sharding import PartitionSpec as P


GRID = 40
ROWS = GRID * GRID
LANES = 128
HALF = 64
PIECES = 32
PIECE = GRID**3 // PIECES
GROUPS = PIECE // GRID
TILES = -(-PIECE // LANES)
WIDE = TILES * LANES
FLAT = GRID**3 // LANES
CYCLE = 8
PARTS = 4
STEPS = 2
ROUNDS = ({0: 0, 2: 2, 3: 3}, {2: 0, 3: 1}, {0: 1, 1: 0}, {0: 2, 1: 3, 2: 1, 3: 0}, {0: 3, 1: 2}, {1: 1, 2: 3, 3: 2})
BLOCK = 8
SCREEN = 0.3


def tables():
    index = np.arange(GRID)
    product = index[:, None] * index[None, :] % GRID
    folded = np.minimum(product, GRID - product)
    angle = 2.0 * math.pi / GRID * folded
    cos = np.cos(angle)
    sin = np.where(product <= GRID // 2, 1.0, -1.0) * np.sin(angle)
    sin = np.where((product == 0) | (product == GRID // 2), 0.0, sin)
    return cos.astype(np.float32), sin.astype(np.float32)


def weights():
    cos, sin = tables()

    def left(sign):
        return np.block([[cos, sign * sin], [-sign * sin, cos]])

    first = np.zeros((2 * LANES, 2 * LANES), np.float32)
    spread = np.zeros((2 * LANES, 2 * LANES), np.float32)
    for plane in range(2):
        for row, col, cosine, sine in ((0, 0, cos, 0.0), (0, 1, 0.0, -sin), (1, 0, 0.0, sin), (1, 1, cos, 0.0)):
            near, far = plane * LANES + row * HALF, col * LANES + plane * HALF
            first[near : near + GRID, far : far + GRID] = cosine + sine
        for row, col, cosine, sine in ((0, 0, cos, 0.0), (0, 1, 0.0, sin), (1, 0, 0.0, -sin), (1, 1, cos, 0.0)):
            near, far = row * LANES + plane * HALF, plane * LANES + col * HALF
            spread[near : near + GRID, far : far + GRID] = cosine + sine
    return left(1.0), left(-1.0), first, spread


def kernel_table():
    index = jnp.arange(GRID, dtype=jnp.int32)
    wrapped = (index + GRID // 2) % GRID - GRID // 2
    wave = 2.0 * math.pi / GRID * wrapped.astype(jnp.float32)
    square = wave * wave
    lane = jnp.arange(LANES, dtype=jnp.int32) % GRID
    lane_wrapped = (lane + GRID // 2) % GRID - GRID // 2
    lane_wave = 2.0 * math.pi / GRID * lane_wrapped.astype(jnp.float32)
    lane_square = lane_wave * lane_wave
    total = square[None, :, None] + square[:, None, None] + lane_square[None, None, :]
    return 4.0 * math.pi / (total + SCREEN * SCREEN) / float(GRID**3)


def gather_body(flat_ref, out_ref, raw, rows, pieces, ready, arrived, left):
    copy = pltpu.make_async_copy(flat_ref, raw, arrived)
    copy.start()
    copy.wait()
    lane = lax.broadcasted_iota(jnp.int32, (PIECES // CYCLE, LANES), 1)
    period = CYCLE * PIECE // LANES
    rows[:FLAT, :] = raw[...].astype(jnp.float32).reshape(FLAT, LANES)
    rows[FLAT:, :] = jnp.zeros((rows.shape[0] - FLAT, LANES), jnp.float32)
    for piece in range(CYCLE):
        for tile in range(TILES):
            row, shift = divmod(PIECE * piece + LANES * tile, LANES)
            value = rows[pl.ds(row, PIECES // CYCLE, stride=period), :]
            if shift:
                after = rows[pl.ds(row + 1, PIECES // CYCLE, stride=period), :]
                value = pltpu.roll(jnp.where(lane >= shift, value, after), LANES - shift, 1)
            pieces[tile, pl.ds(piece, PIECES // CYCLE, stride=CYCLE), :] = value
    for tile in range(TILES):
        ready[:, tile * LANES : (tile + 1) * LANES] = pieces[tile].astype(jnp.bfloat16)
    copy = pltpu.make_async_copy(ready, out_ref, left)
    copy.start()
    copy.wait()


def body(own_ref, came_ref, t_ref, kern_ref, fwd_ref, inv_ref, first_ref, last_ref, out_ref, xs, near, real, imag, real_back, imag_back, back, ys, flat, sums):
    lane = lax.broadcasted_iota(jnp.int32, (PIECES, LANES), 1)
    low = lane < HALF

    target = t_ref[...]
    flat[0] = own_ref[...] * target
    flat[1] = came_ref[...] * target

    def aligned(which, group, to):
        start = GRID * group
        tile, shift = start // LANES, start % LANES
        value = flat[which, :, tile * LANES : (tile + 1) * LANES]
        if shift + GRID > LANES:
            after = flat[which, :, (tile + 1) * LANES : (tile + 2) * LANES]
            value = jnp.where(lane >= shift, value, after)
        turn = (to - shift) % LANES
        return pltpu.roll(value, turn, 1) if turn else value

    for group in range(GROUPS):
        merged = jnp.where(low, aligned(0, group, 0), aligned(1, group, HALF))
        xs[pl.ds(group, PIECES, stride=GROUPS), :] = merged.astype(jnp.float32)

    forward, inverse = fwd_ref[...], inv_ref[...]
    re, im = slice(0, LANES), slice(LANES, 2 * LANES)

    def turned(table, first, second):
        both = jnp.concatenate([first, second], axis=1).astype(jnp.bfloat16)
        return jnp.dot(table, both, preferred_element_type=jnp.float32)

    def stacked(rows):
        return jnp.concatenate([real[rows, :], imag[rows, :]], axis=0)

    def put(refs, rows, value):
        refs[0][rows, :] = value[:GRID]
        refs[1][rows, :] = value[GRID:]

    def plane(index):
        return pl.ds(index * GRID, GRID)

    def paired(index):
        rows, far = plane(index), plane(index + GRID // 2)
        both = [jnp.where(low_rows, ref[rows, :], pltpu.roll(ref[far, :], HALF, 1)) for ref in (real_back, imag_back)]
        return jnp.concatenate(both, axis=0)

    low_rows = lax.broadcasted_iota(jnp.int32, (GRID, LANES), 1) < HALF

    def along_c(source, table_ref, result, step):
        size = ROWS // 2 // STEPS
        one, two = pl.ds(step * size, size), pl.ds(ROWS // 2 + step * size, size)
        both = jnp.concatenate([source[one, :], source[two, :]], axis=1).astype(jnp.bfloat16)
        value = jnp.dot(both, table_ref[...], preferred_element_type=jnp.float32)
        result[one, :] = value[:, re]
        result[two, :] = value[:, im]

    pairs = GRID // 4 // STEPS
    for step in range(STEPS):
        along_c(xs, first_ref, near, step)
    for step in range(STEPS):
        for pair in range(step * pairs, (step + 1) * pairs):
            chosen = (2 * pair, 2 * pair + 1)
            slabs = [jnp.concatenate([near[plane(index), :], near[plane(index + GRID // 2), :]], axis=0) for index in chosen]
            value = turned(forward, *slabs)
            for index, part in zip(chosen, (re, im), strict=True):
                put((real, imag), plane(index), value[:, part])
                put((real, imag), plane(index + GRID // 2), pltpu.roll(value[:, part], HALF, 1))
    for pair in range(GRID // 2):
        one, two = pl.ds(2 * pair, GRID, stride=GRID), pl.ds(2 * pair + 1, GRID, stride=GRID)
        value = turned(forward, stacked(one), stacked(two))
        scale = [jnp.concatenate([kern_ref[2 * pair + which]] * 2, axis=0) for which in range(2)]
        value = turned(inverse, value[:, re] * scale[0], value[:, im] * scale[1])
        put((real_back, imag_back), one, value[:, re])
        put((real_back, imag_back), two, value[:, im])
    for step in range(STEPS):
        for pair in range(step * pairs, (step + 1) * pairs):
            value = turned(inverse, paired(2 * pair), paired(2 * pair + 1))
            for index, part in ((2 * pair, re), (2 * pair + 1, im)):
                back[plane(index), :] = value[:GRID, part]
                back[plane(index + GRID // 2), :] = value[GRID:, part]
    for step in range(STEPS):
        along_c(back, last_ref, ys, step)

    tiles = [[None] * TILES for _ in range(2)]
    for group in range(GROUPS):
        start = GRID * group
        tile, shift = start // LANES, start % LANES
        value = ys[pl.ds(group, PIECES, stride=GROUPS), :].astype(jnp.bfloat16)
        for which in range(2):
            turn = (shift - HALF * which) % LANES
            moved = pltpu.roll(value, turn, 1) if turn else value
            held = tiles[which][tile]
            tiles[which][tile] = moved if held is None else jnp.where(lane >= shift, moved, held)
            if shift + GRID > LANES:
                tiles[which][tile + 1] = moved
    for tile in range(TILES):
        here = slice(tile * LANES, (tile + 1) * LANES)
        total = own_ref[:, here].astype(jnp.float32) * tiles[0][tile].astype(jnp.float32)
        total += came_ref[:, here].astype(jnp.float32) * tiles[1][tile].astype(jnp.float32)
        for part in range(PARTS):
            sums[pl.ds(part * TILES + tile, BLOCK, stride=PARTS * TILES), :] = -total[part * BLOCK : (part + 1) * BLOCK]
    out_ref[...] = sums[...].astype(jnp.bfloat16)


VMEM = pl.BlockSpec(memory_space=pltpu.VMEM)
PARAMS = pltpu.CompilerParams(vmem_limit_bytes=16 * 2**20)


def gathered(block):
    return pl.pallas_call(
        gather_body,
        out_shape=jax.ShapeDtypeStruct((PIECES, WIDE), jnp.bfloat16),
        in_specs=[pl.BlockSpec(memory_space=pltpu.HBM)],
        out_specs=pl.BlockSpec(memory_space=pltpu.HBM),
        scratch_shapes=[
            pltpu.VMEM((1, GRID**3), jnp.bfloat16),
            pltpu.VMEM((FLAT + 4, LANES), jnp.float32),
            pltpu.VMEM((TILES, PIECES, LANES), jnp.float32),
            pltpu.VMEM((PIECES, WIDE), jnp.bfloat16),
            pltpu.SemaphoreType.DMA,
            pltpu.SemaphoreType.DMA,
        ],
        compiler_params=pltpu.CompilerParams(vmem_limit_bytes=61000 * 1024),
        cost_estimate=pl.CostEstimate(flops=1_000_000, bytes_accessed=800_000, transcendentals=0),
        name="gather",
    )(block)


def exchange_term(own, came, target):
    constants = [jnp.asarray(w, jnp.bfloat16) for w in weights()]
    return pl.pallas_call(
        body,
        out_shape=jax.ShapeDtypeStruct((PIECES * TILES, LANES), jnp.bfloat16),
        in_specs=[VMEM] * 8,
        out_specs=VMEM,
        scratch_shapes=[
            *[pltpu.VMEM((ROWS, LANES), jnp.float32)] * 8,
            pltpu.VMEM((2, PIECES, WIDE), jnp.bfloat16),
            pltpu.VMEM((PIECES * TILES, LANES), jnp.float32),
        ],
        compiler_params=PARAMS,
        cost_estimate=pl.CostEstimate(flops=200_000_000, bytes_accessed=2_000_000, transcendentals=0),
        name="exchange",
    )(own, came, target, kernel_table(), *constants)


def from_ahead(block):
    count = lax.axis_size("blk")
    return lax.ppermute(block, "blk", [((i + 1) % count, i) for i in range(count)])


def block_sum_body(came_ref, *refs):
    *out_refs, held = refs
    total = came_ref[0].astype(jnp.float32)
    for other in range(1, BLOCK):
        total += came_ref[other].astype(jnp.float32)
    held[...] = total
    part = lax.div(lax.axis_index("wide"), BLOCK)
    for ends, out_ref in zip(ROUNDS, out_refs, strict=True):
        end = jnp.int32(0)
        for start, chosen in ends.items():
            end = jnp.where(part == start, chosen, end)
        out_ref[...] = held[pl.ds(pl.multiple_of(end * TILES, TILES), TILES), :].astype(jnp.bfloat16)


def block_sum(came):
    shape = (TILES, LANES)
    return pl.pallas_call(
        block_sum_body,
        out_shape=[jax.ShapeDtypeStruct(shape, jnp.bfloat16)] * len(ROUNDS),
        in_specs=[VMEM],
        out_specs=[VMEM] * len(ROUNDS),
        scratch_shapes=[pltpu.VMEM((PARTS * TILES, LANES), jnp.float32)],
        compiler_params=PARAMS,
        cost_estimate=pl.CostEstimate(flops=100_000, bytes_accessed=150_000, transcendentals=0),
        name="block_sum",
    )(came)


def last_sum_body(*refs):
    total = refs[0][...].astype(jnp.float32)
    for ref in refs[1:-1]:
        total += ref[...].astype(jnp.float32)
    refs[-1][...] = total


def last_sum(came):
    return pl.pallas_call(
        last_sum_body,
        out_shape=jax.ShapeDtypeStruct((TILES, LANES), jnp.float32),
        in_specs=[VMEM] * len(came),
        out_specs=VMEM,
        compiler_params=PARAMS,
        cost_estimate=pl.CostEstimate(flops=100_000, bytes_accessed=80_000, transcendentals=0),
        name="last_sum",
    )(*came)


def shards(sources, targets):
    blk = lax.axis_size("blk")
    own = gathered(sources)
    partial = exchange_term(own, from_ahead(own), gathered(targets))
    groups = [[part * BLOCK + i for i in range(BLOCK)] for part in range(PARTS)]
    came = lax.all_to_all(partial, "wide", split_axis=0, concat_axis=0, axis_index_groups=groups, tiled=True)
    sent = block_sum(came.reshape(BLOCK, PARTS * TILES, LANES))
    arrived = []
    for turn, ends in enumerate(ROUNDS):
        pairs = [(start * BLOCK + i, end * BLOCK + i) for start, end in ends.items() for i in range(BLOCK)]
        route = [(near * blk + b, far * blk + (b + 1) % blk) for near, far in pairs for b in range(blk)]
        arrived.append(lax.ppermute(sent[turn], ("wide", "blk"), route))
    return last_sum(arrived).reshape(1, -1)[:, :PIECE]


def solution(mesh):
    in_specs = (P(("wide", "blk"), None), P("blk", None))
    return jax.shard_map(shards, mesh=mesh, in_specs=in_specs, out_specs=P("blk", "wide"), check_vma=False)
```

```python
import math

import jax
import jax.numpy as jnp
import numpy as np
from jax import lax
from jax.experimental import pallas as pl
from jax.experimental.pallas import tpu as pltpu
from jax.sharding import PartitionSpec as P


GRID = 40
ROWS = GRID * GRID
LANES = 128
HALF = 64
PIECES = 32
PIECE = GRID**3 // PIECES
GROUPS = PIECE // GRID
TILES = -(-PIECE // LANES)
WIDE = TILES * LANES
FLAT = GRID**3 // LANES
CYCLE = 8
PARTS = 4
STEPS = 2
ROUNDS = ({0: 0, 2: 2, 3: 3}, {2: 0, 3: 1}, {0: 1, 1: 0}, {0: 2, 1: 3, 2: 1, 3: 0}, {0: 3, 1: 2}, {1: 1, 2: 3, 3: 2})
BLOCK = 8
SCREEN = 0.3


def tables():
    index = np.arange(GRID)
    product = index[:, None] * index[None, :] % GRID
    folded = np.minimum(product, GRID - product)
    angle = 2.0 * math.pi / GRID * folded
    cos = np.cos(angle)
    sin = np.where(product <= GRID // 2, 1.0, -1.0) * np.sin(angle)
    sin = np.where((product == 0) | (product == GRID // 2), 0.0, sin)
    return cos.astype(np.float32), sin.astype(np.float32)


def weights():
    cos, sin = tables()

    def left(sign):
        return np.block([[cos, sign * sin], [-sign * sin, cos]])

    first = np.zeros((2 * LANES, 2 * LANES), np.float32)
    spread = np.zeros((2 * LANES, 2 * LANES), np.float32)
    for plane in range(2):
        for row, col, cosine, sine in ((0, 0, cos, 0.0), (0, 1, 0.0, -sin), (1, 0, 0.0, sin), (1, 1, cos, 0.0)):
            near, far = plane * LANES + row * HALF, col * LANES + plane * HALF
            first[near : near + GRID, far : far + GRID] = cosine + sine
        for row, col, cosine, sine in ((0, 0, cos, 0.0), (0, 1, 0.0, sin), (1, 0, 0.0, -sin), (1, 1, cos, 0.0)):
            near, far = row * LANES + plane * HALF, plane * LANES + col * HALF
            spread[near : near + GRID, far : far + GRID] = cosine + sine
    return left(1.0), left(-1.0), first, spread


def kernel_table():
    index = jnp.arange(GRID, dtype=jnp.int32)
    wrapped = (index + GRID // 2) % GRID - GRID // 2
    wave = 2.0 * math.pi / GRID * wrapped.astype(jnp.float32)
    square = wave * wave
    lane = jnp.arange(LANES, dtype=jnp.int32) % GRID
    lane_wrapped = (lane + GRID // 2) % GRID - GRID // 2
    lane_wave = 2.0 * math.pi / GRID * lane_wrapped.astype(jnp.float32)
    lane_square = lane_wave * lane_wave
    total = square[None, :, None] + square[:, None, None] + lane_square[None, None, :]
    return 4.0 * math.pi / (total + SCREEN * SCREEN) / float(GRID**3)


def gather_body(flat_ref, out_ref, raw, rows, pieces, ready, arrived, left):
    copy = pltpu.make_async_copy(flat_ref, raw, arrived)
    copy.start()
    copy.wait()
    lane = lax.broadcasted_iota(jnp.int32, (PIECES // CYCLE, LANES), 1)
    period = CYCLE * PIECE // LANES
    rows[:FLAT, :] = raw[...].astype(jnp.float32).reshape(FLAT, LANES)
    rows[FLAT:, :] = jnp.zeros((rows.shape[0] - FLAT, LANES), jnp.float32)
    for piece in range(CYCLE):
        for tile in range(TILES):
            row, shift = divmod(PIECE * piece + LANES * tile, LANES)
            value = rows[pl.ds(row, PIECES // CYCLE, stride=period), :]
            if shift:
                after = rows[pl.ds(row + 1, PIECES // CYCLE, stride=period), :]
                value = pltpu.roll(jnp.where(lane >= shift, value, after), LANES - shift, 1)
            pieces[tile, pl.ds(piece, PIECES // CYCLE, stride=CYCLE), :] = value
    for tile in range(TILES):
        ready[:, tile * LANES : (tile + 1) * LANES] = pieces[tile].astype(jnp.bfloat16)
    copy = pltpu.make_async_copy(ready, out_ref, left)
    copy.start()
    copy.wait()


def body(own_ref, came_ref, t_ref, kern_ref, fwd_ref, inv_ref, first_ref, last_ref, out_ref, xs, near, real, imag, real_back, imag_back, back, ys, flat, sums):
    lane = lax.broadcasted_iota(jnp.int32, (PIECES, LANES), 1)

    target = t_ref[...]
    flat[0] = own_ref[...] * target
    flat[1] = came_ref[...] * target

    turned_lane = lax.rem(lane + HALF, LANES)
    for tile in range(TILES):
        here = slice(tile * LANES, (tile + 1) * LANES)
        flat[1, :, here] = pltpu.roll(flat[1, :, here], HALF, 1)

    def window(which, tile, shift, place):
        value = flat[which, :, tile * LANES : (tile + 1) * LANES]
        if shift + GRID > LANES:
            value = jnp.where(place >= shift, value, flat[which, :, (tile + 1) * LANES : (tile + 2) * LANES])
        return value

    for group in range(GROUPS):
        tile, shift = divmod(GRID * group, LANES)
        first_half = lax.rem(lane + (LANES - shift), LANES) < HALF
        merged = jnp.where(first_half, window(0, tile, shift, lane), window(1, tile, shift, turned_lane))
        if shift:
            merged = pltpu.roll(merged, LANES - shift, 1)
        xs[pl.ds(group, PIECES, stride=GROUPS), :] = merged.astype(jnp.float32)

    forward, inverse = fwd_ref[...], inv_ref[...]
    re, im = slice(0, LANES), slice(LANES, 2 * LANES)

    def turned(table, first, second):
        both = jnp.concatenate([first, second], axis=1).astype(jnp.bfloat16)
        return jnp.dot(table, both, preferred_element_type=jnp.float32)

    def stacked(rows):
        return jnp.concatenate([real[rows, :], imag[rows, :]], axis=0)

    def put(refs, rows, value):
        refs[0][rows, :] = value[:GRID]
        refs[1][rows, :] = value[GRID:]

    def plane(index):
        return pl.ds(index * GRID, GRID)

    def paired(index):
        rows, far = plane(index), plane(index + GRID // 2)
        both = [jnp.where(low_rows, ref[rows, :], pltpu.roll(ref[far, :], HALF, 1)) for ref in (real_back, imag_back)]
        return jnp.concatenate(both, axis=0)

    low_rows = lax.broadcasted_iota(jnp.int32, (GRID, LANES), 1) < HALF

    def along_c(source, table_ref, result, step):
        size = ROWS // 2 // STEPS
        one, two = pl.ds(step * size, size), pl.ds(ROWS // 2 + step * size, size)
        both = jnp.concatenate([source[one, :], source[two, :]], axis=1).astype(jnp.bfloat16)
        value = jnp.dot(both, table_ref[...], preferred_element_type=jnp.float32)
        result[one, :] = value[:, re]
        result[two, :] = value[:, im]

    pairs = GRID // 4 // STEPS
    for step in range(STEPS):
        along_c(xs, first_ref, near, step)
    for step in range(STEPS):
        for pair in range(step * pairs, (step + 1) * pairs):
            chosen = (2 * pair, 2 * pair + 1)
            slabs = [jnp.concatenate([near[plane(index), :], near[plane(index + GRID // 2), :]], axis=0) for index in chosen]
            value = turned(forward, *slabs)
            for index, part in zip(chosen, (re, im), strict=True):
                put((real, imag), plane(index), value[:, part])
                put((real, imag), plane(index + GRID // 2), pltpu.roll(value[:, part], HALF, 1))
    for pair in range(GRID // 2):
        one, two = pl.ds(2 * pair, GRID, stride=GRID), pl.ds(2 * pair + 1, GRID, stride=GRID)
        value = turned(forward, stacked(one), stacked(two))
        scale = [jnp.concatenate([kern_ref[2 * pair + which]] * 2, axis=0) for which in range(2)]
        value = turned(inverse, value[:, re] * scale[0], value[:, im] * scale[1])
        put((real_back, imag_back), one, value[:, re])
        put((real_back, imag_back), two, value[:, im])
    for step in range(STEPS):
        for pair in range(step * pairs, (step + 1) * pairs):
            value = turned(inverse, paired(2 * pair), paired(2 * pair + 1))
            for index, part in ((2 * pair, re), (2 * pair + 1, im)):
                back[plane(index), :] = value[:GRID, part]
                back[plane(index + GRID // 2), :] = value[GRID:, part]
    for step in range(STEPS):
        along_c(back, last_ref, ys, step)

    tiles = [[None] * TILES for _ in range(2)]
    for group in range(GROUPS):
        start = GRID * group
        tile, shift = start // LANES, start % LANES
        value = ys[pl.ds(group, PIECES, stride=GROUPS), :].astype(jnp.bfloat16)
        for which in range(2):
            turn = (shift - HALF * which) % LANES
            moved = pltpu.roll(value, turn, 1) if turn else value
            held = tiles[which][tile]
            tiles[which][tile] = moved if held is None else jnp.where(lane >= shift, moved, held)
            if shift + GRID > LANES:
                tiles[which][tile + 1] = moved
    for tile in range(TILES):
        here = slice(tile * LANES, (tile + 1) * LANES)
        total = own_ref[:, here].astype(jnp.float32) * tiles[0][tile].astype(jnp.float32)
        total += came_ref[:, here].astype(jnp.float32) * tiles[1][tile].astype(jnp.float32)
        for part in range(PARTS):
            sums[pl.ds(part * TILES + tile, BLOCK, stride=PARTS * TILES), :] = -total[part * BLOCK : (part + 1) * BLOCK]
    out_ref[...] = sums[...].astype(jnp.bfloat16)


VMEM = pl.BlockSpec(memory_space=pltpu.VMEM)
PARAMS = pltpu.CompilerParams(vmem_limit_bytes=16 * 2**20)


def gathered(block):
    return pl.pallas_call(
        gather_body,
        out_shape=jax.ShapeDtypeStruct((PIECES, WIDE), jnp.bfloat16),
        in_specs=[pl.BlockSpec(memory_space=pltpu.HBM)],
        out_specs=pl.BlockSpec(memory_space=pltpu.HBM),
        scratch_shapes=[
            pltpu.VMEM((1, GRID**3), jnp.bfloat16),
            pltpu.VMEM((FLAT + 4, LANES), jnp.float32),
            pltpu.VMEM((TILES, PIECES, LANES), jnp.float32),
            pltpu.VMEM((PIECES, WIDE), jnp.bfloat16),
            pltpu.SemaphoreType.DMA,
            pltpu.SemaphoreType.DMA,
        ],
        compiler_params=pltpu.CompilerParams(vmem_limit_bytes=61000 * 1024),
        cost_estimate=pl.CostEstimate(flops=1_000_000, bytes_accessed=800_000, transcendentals=0),
        name="gather",
    )(block)


def exchange_term(own, came, target):
    constants = [jnp.asarray(w, jnp.bfloat16) for w in weights()]
    return pl.pallas_call(
        body,
        out_shape=jax.ShapeDtypeStruct((PIECES * TILES, LANES), jnp.bfloat16),
        in_specs=[VMEM] * 8,
        out_specs=VMEM,
        scratch_shapes=[
            *[pltpu.VMEM((ROWS, LANES), jnp.float32)] * 8,
            pltpu.VMEM((2, PIECES, WIDE), jnp.bfloat16),
            pltpu.VMEM((PIECES * TILES, LANES), jnp.float32),
        ],
        compiler_params=PARAMS,
        cost_estimate=pl.CostEstimate(flops=200_000_000, bytes_accessed=2_000_000, transcendentals=0),
        name="exchange",
    )(own, came, target, kernel_table(), *constants)


def from_ahead(block):
    count = lax.axis_size("blk")
    return lax.ppermute(block, "blk", [((i + 1) % count, i) for i in range(count)])


def block_sum_body(came_ref, *refs):
    *out_refs, held = refs
    total = came_ref[0].astype(jnp.float32)
    for other in range(1, BLOCK):
        total += came_ref[other].astype(jnp.float32)
    held[...] = total
    part = lax.div(lax.axis_index("wide"), BLOCK)
    for ends, out_ref in zip(ROUNDS, out_refs, strict=True):
        end = jnp.int32(0)
        for start, chosen in ends.items():
            end = jnp.where(part == start, chosen, end)
        out_ref[...] = held[pl.ds(pl.multiple_of(end * TILES, TILES), TILES), :].astype(jnp.bfloat16)


def block_sum(came):
    shape = (TILES, LANES)
    return pl.pallas_call(
        block_sum_body,
        out_shape=[jax.ShapeDtypeStruct(shape, jnp.bfloat16)] * len(ROUNDS),
        in_specs=[VMEM],
        out_specs=[VMEM] * len(ROUNDS),
        scratch_shapes=[pltpu.VMEM((PARTS * TILES, LANES), jnp.float32)],
        compiler_params=PARAMS,
        cost_estimate=pl.CostEstimate(flops=100_000, bytes_accessed=150_000, transcendentals=0),
        name="block_sum",
    )(came)


def last_sum_body(*refs):
    total = refs[0][...].astype(jnp.float32)
    for ref in refs[1:-1]:
        total += ref[...].astype(jnp.float32)
    refs[-1][...] = total


def last_sum(came):
    return pl.pallas_call(
        last_sum_body,
        out_shape=jax.ShapeDtypeStruct((TILES, LANES), jnp.float32),
        in_specs=[VMEM] * len(came),
        out_specs=VMEM,
        compiler_params=PARAMS,
        cost_estimate=pl.CostEstimate(flops=100_000, bytes_accessed=80_000, transcendentals=0),
        name="last_sum",
    )(*came)


def shards(sources, targets):
    blk = lax.axis_size("blk")
    own = gathered(sources)
    partial = exchange_term(own, from_ahead(own), gathered(targets))
    groups = [[part * BLOCK + i for i in range(BLOCK)] for part in range(PARTS)]
    came = lax.all_to_all(partial, "wide", split_axis=0, concat_axis=0, axis_index_groups=groups, tiled=True)
    sent = block_sum(came.reshape(BLOCK, PARTS * TILES, LANES))
    arrived = []
    for turn, ends in enumerate(ROUNDS):
        pairs = [(start * BLOCK + i, end * BLOCK + i) for start, end in ends.items() for i in range(BLOCK)]
        route = [(near * blk + b, far * blk + (b + 1) % blk) for near, far in pairs for b in range(blk)]
        arrived.append(lax.ppermute(sent[turn], ("wide", "blk"), route))
    return last_sum(arrived).reshape(1, -1)[:, :PIECE]


def solution(mesh):
    in_specs = (P(("wide", "blk"), None), P("blk", None))
    return jax.shard_map(shards, mesh=mesh, in_specs=in_specs, out_specs=P("blk", "wide"), check_vma=False)
```

```python
import math

import jax
import jax.numpy as jnp
import numpy as np
from jax import lax
from jax.experimental import pallas as pl
from jax.experimental.pallas import tpu as pltpu
from jax.sharding import PartitionSpec as P


GRID = 40
ROWS = GRID * GRID
LANES = 128
HALF = 64
PIECES = 32
PIECE = GRID**3 // PIECES
GROUPS = PIECE // GRID
TILES = -(-PIECE // LANES)
WIDE = TILES * LANES
FLAT = GRID**3 // LANES
CYCLE = 8
PARTS = 4
STEPS = 2
ROUNDS = ({0: 0, 2: 2, 3: 3}, {2: 0, 3: 1}, {0: 1, 1: 0}, {0: 2, 1: 3, 2: 1, 3: 0}, {0: 3, 1: 2}, {1: 1, 2: 3, 3: 2})
BLOCK = 8
SCREEN = 0.3


def tables():
    index = np.arange(GRID)
    product = index[:, None] * index[None, :] % GRID
    folded = np.minimum(product, GRID - product)
    angle = 2.0 * math.pi / GRID * folded
    cos = np.cos(angle)
    sin = np.where(product <= GRID // 2, 1.0, -1.0) * np.sin(angle)
    sin = np.where((product == 0) | (product == GRID // 2), 0.0, sin)
    return cos.astype(np.float32), sin.astype(np.float32)


def weights():
    cos, sin = tables()

    def left(sign):
        return np.block([[cos, sign * sin], [-sign * sin, cos]])

    first = np.zeros((2 * LANES, 2 * LANES), np.float32)
    spread = np.zeros((2 * LANES, 2 * LANES), np.float32)
    for plane in range(2):
        for row, col, cosine, sine in ((0, 0, cos, 0.0), (0, 1, 0.0, -sin), (1, 0, 0.0, sin), (1, 1, cos, 0.0)):
            near, far = plane * LANES + row * HALF, col * LANES + plane * HALF
            first[near : near + GRID, far : far + GRID] = cosine + sine
        for row, col, cosine, sine in ((0, 0, cos, 0.0), (0, 1, 0.0, sin), (1, 0, 0.0, -sin), (1, 1, cos, 0.0)):
            near, far = row * LANES + plane * HALF, plane * LANES + col * HALF
            spread[near : near + GRID, far : far + GRID] = cosine + sine
    return left(1.0), left(-1.0), first, spread


def kernel_table():
    index = jnp.arange(GRID, dtype=jnp.int32)
    wrapped = (index + GRID // 2) % GRID - GRID // 2
    wave = 2.0 * math.pi / GRID * wrapped.astype(jnp.float32)
    square = wave * wave
    lane = jnp.arange(LANES, dtype=jnp.int32) % GRID
    lane_wrapped = (lane + GRID // 2) % GRID - GRID // 2
    lane_wave = 2.0 * math.pi / GRID * lane_wrapped.astype(jnp.float32)
    lane_square = lane_wave * lane_wave
    total = square[None, :, None] + square[:, None, None] + lane_square[None, None, :]
    return 4.0 * math.pi / (total + SCREEN * SCREEN) / float(GRID**3)


def gather_body(flat_ref, out_ref, raw, rows, pieces, ready, arrived, left):
    copy = pltpu.make_async_copy(flat_ref, raw, arrived)
    copy.start()
    copy.wait()
    lane = lax.broadcasted_iota(jnp.int32, (PIECES // CYCLE, LANES), 1)
    period = CYCLE * PIECE // LANES
    rows[:FLAT, :] = raw[...].astype(jnp.float32).reshape(FLAT, LANES)
    rows[FLAT:, :] = jnp.zeros((rows.shape[0] - FLAT, LANES), jnp.float32)
    copies = []
    for half in range(2):
        chosen = range(half * TILES // 2, (half + 1) * TILES // 2)
        for piece in range(CYCLE):
            for tile in chosen:
                row, shift = divmod(PIECE * piece + LANES * tile, LANES)
                value = rows[pl.ds(row, PIECES // CYCLE, stride=period), :]
                if shift:
                    after = rows[pl.ds(row + 1, PIECES // CYCLE, stride=period), :]
                    value = pltpu.roll(jnp.where(lane >= shift, value, after), LANES - shift, 1)
                pieces[tile, pl.ds(piece, PIECES // CYCLE, stride=CYCLE), :] = value
        for tile in chosen:
            ready[:, tile * LANES : (tile + 1) * LANES] = pieces[tile].astype(jnp.bfloat16)
        here = pl.ds(half * WIDE // 2, WIDE // 2)
        copies.append(pltpu.make_async_copy(ready.at[:, here], out_ref.at[:, here], left.at[half]))
        copies[-1].start()
    for copy in copies:
        copy.wait()


def body(own_ref, came_ref, t_ref, kern_ref, fwd_ref, inv_ref, first_ref, last_ref, out_ref, xs, near, real, imag, real_back, imag_back, back, ys, flat, sums):
    lane = lax.broadcasted_iota(jnp.int32, (PIECES, LANES), 1)

    target = t_ref[...]
    flat[0] = own_ref[...] * target
    flat[1] = came_ref[...] * target

    turned_lane = lax.rem(lane + HALF, LANES)
    for tile in range(TILES):
        here = slice(tile * LANES, (tile + 1) * LANES)
        flat[1, :, here] = pltpu.roll(flat[1, :, here], HALF, 1)

    def window(which, tile, shift, place):
        value = flat[which, :, tile * LANES : (tile + 1) * LANES]
        if shift + GRID > LANES:
            value = jnp.where(place >= shift, value, flat[which, :, (tile + 1) * LANES : (tile + 2) * LANES])
        return value

    for group in range(GROUPS):
        tile, shift = divmod(GRID * group, LANES)
        first_half = lax.rem(lane + (LANES - shift), LANES) < HALF
        merged = jnp.where(first_half, window(0, tile, shift, lane), window(1, tile, shift, turned_lane))
        if shift:
            merged = pltpu.roll(merged, LANES - shift, 1)
        xs[pl.ds(group, PIECES, stride=GROUPS), :] = merged.astype(jnp.float32)

    forward, inverse = fwd_ref[...], inv_ref[...]
    re, im = slice(0, LANES), slice(LANES, 2 * LANES)

    def turned(table, first, second):
        both = jnp.concatenate([first, second], axis=1).astype(jnp.bfloat16)
        return jnp.dot(table, both, preferred_element_type=jnp.float32)

    def stacked(rows):
        return jnp.concatenate([real[rows, :], imag[rows, :]], axis=0)

    def put(refs, rows, value):
        refs[0][rows, :] = value[:GRID]
        refs[1][rows, :] = value[GRID:]

    def plane(index):
        return pl.ds(index * GRID, GRID)

    def paired(index):
        rows, far = plane(index), plane(index + GRID // 2)
        both = [jnp.where(low_rows, ref[rows, :], pltpu.roll(ref[far, :], HALF, 1)) for ref in (real_back, imag_back)]
        return jnp.concatenate(both, axis=0)

    low_rows = lax.broadcasted_iota(jnp.int32, (GRID, LANES), 1) < HALF

    def along_c(source, table_ref, result, step):
        size = ROWS // 2 // STEPS
        one, two = pl.ds(step * size, size), pl.ds(ROWS // 2 + step * size, size)
        both = jnp.concatenate([source[one, :], source[two, :]], axis=1).astype(jnp.bfloat16)
        value = jnp.dot(both, table_ref[...], preferred_element_type=jnp.float32)
        result[one, :] = value[:, re]
        result[two, :] = value[:, im]

    pairs = GRID // 4 // STEPS
    for step in range(STEPS):
        along_c(xs, first_ref, near, step)
    for step in range(STEPS):
        for pair in range(step * pairs, (step + 1) * pairs):
            chosen = (2 * pair, 2 * pair + 1)
            slabs = [jnp.concatenate([near[plane(index), :], near[plane(index + GRID // 2), :]], axis=0) for index in chosen]
            value = turned(forward, *slabs)
            for index, part in zip(chosen, (re, im), strict=True):
                put((real, imag), plane(index), value[:, part])
                put((real, imag), plane(index + GRID // 2), pltpu.roll(value[:, part], HALF, 1))
    for pair in range(GRID // 2):
        one, two = pl.ds(2 * pair, GRID, stride=GRID), pl.ds(2 * pair + 1, GRID, stride=GRID)
        value = turned(forward, stacked(one), stacked(two))
        scale = [jnp.concatenate([kern_ref[2 * pair + which]] * 2, axis=0) for which in range(2)]
        value = turned(inverse, value[:, re] * scale[0], value[:, im] * scale[1])
        put((real_back, imag_back), one, value[:, re])
        put((real_back, imag_back), two, value[:, im])
    for step in range(STEPS):
        for pair in range(step * pairs, (step + 1) * pairs):
            value = turned(inverse, paired(2 * pair), paired(2 * pair + 1))
            for index, part in ((2 * pair, re), (2 * pair + 1, im)):
                back[plane(index), :] = value[:GRID, part]
                back[plane(index + GRID // 2), :] = value[GRID:, part]
    for step in range(STEPS):
        along_c(back, last_ref, ys, step)

    tiles = [[None] * TILES for _ in range(2)]
    for group in range(GROUPS):
        start = GRID * group
        tile, shift = start // LANES, start % LANES
        value = ys[pl.ds(group, PIECES, stride=GROUPS), :].astype(jnp.bfloat16)
        for which in range(2):
            turn = (shift - HALF * which) % LANES
            moved = pltpu.roll(value, turn, 1) if turn else value
            held = tiles[which][tile]
            tiles[which][tile] = moved if held is None else jnp.where(lane >= shift, moved, held)
            if shift + GRID > LANES:
                tiles[which][tile + 1] = moved
    for tile in range(TILES):
        here = slice(tile * LANES, (tile + 1) * LANES)
        total = own_ref[:, here].astype(jnp.float32) * tiles[0][tile].astype(jnp.float32)
        total += came_ref[:, here].astype(jnp.float32) * tiles[1][tile].astype(jnp.float32)
        for part in range(PARTS):
            sums[pl.ds(part * TILES + tile, BLOCK, stride=PARTS * TILES), :] = -total[part * BLOCK : (part + 1) * BLOCK]
    out_ref[...] = sums[...].astype(jnp.bfloat16)


VMEM = pl.BlockSpec(memory_space=pltpu.VMEM)
PARAMS = pltpu.CompilerParams(vmem_limit_bytes=16 * 2**20)


def gathered(block):
    return pl.pallas_call(
        gather_body,
        out_shape=jax.ShapeDtypeStruct((PIECES, WIDE), jnp.bfloat16),
        in_specs=[pl.BlockSpec(memory_space=pltpu.HBM)],
        out_specs=pl.BlockSpec(memory_space=pltpu.HBM),
        scratch_shapes=[
            pltpu.VMEM((1, GRID**3), jnp.bfloat16),
            pltpu.VMEM((FLAT + 4, LANES), jnp.float32),
            pltpu.VMEM((TILES, PIECES, LANES), jnp.float32),
            pltpu.VMEM((PIECES, WIDE), jnp.bfloat16),
            pltpu.SemaphoreType.DMA,
            pltpu.SemaphoreType.DMA((2,)),
        ],
        compiler_params=pltpu.CompilerParams(vmem_limit_bytes=61000 * 1024),
        cost_estimate=pl.CostEstimate(flops=1_000_000, bytes_accessed=800_000, transcendentals=0),
        name="gather",
    )(block)


def exchange_term(own, came, target):
    constants = [jnp.asarray(w, jnp.bfloat16) for w in weights()]
    return pl.pallas_call(
        body,
        out_shape=jax.ShapeDtypeStruct((PIECES * TILES, LANES), jnp.bfloat16),
        in_specs=[VMEM] * 8,
        out_specs=VMEM,
        scratch_shapes=[
            *[pltpu.VMEM((ROWS, LANES), jnp.float32)] * 8,
            pltpu.VMEM((2, PIECES, WIDE), jnp.bfloat16),
            pltpu.VMEM((PIECES * TILES, LANES), jnp.float32),
        ],
        compiler_params=PARAMS,
        cost_estimate=pl.CostEstimate(flops=200_000_000, bytes_accessed=2_000_000, transcendentals=0),
        name="exchange",
    )(own, came, target, kernel_table(), *constants)


def from_ahead(block):
    count = lax.axis_size("blk")
    return lax.ppermute(block, "blk", [((i + 1) % count, i) for i in range(count)])


def block_sum_body(came_ref, *refs):
    *out_refs, held = refs
    total = came_ref[0].astype(jnp.float32)
    for other in range(1, BLOCK):
        total += came_ref[other].astype(jnp.float32)
    held[...] = total
    part = lax.div(lax.axis_index("wide"), BLOCK)
    for ends, out_ref in zip(ROUNDS, out_refs, strict=True):
        end = jnp.int32(0)
        for start, chosen in ends.items():
            end = jnp.where(part == start, chosen, end)
        out_ref[...] = held[pl.ds(pl.multiple_of(end * TILES, TILES), TILES), :].astype(jnp.bfloat16)


def block_sum(came):
    shape = (TILES, LANES)
    return pl.pallas_call(
        block_sum_body,
        out_shape=[jax.ShapeDtypeStruct(shape, jnp.bfloat16)] * len(ROUNDS),
        in_specs=[VMEM],
        out_specs=[VMEM] * len(ROUNDS),
        scratch_shapes=[pltpu.VMEM((PARTS * TILES, LANES), jnp.float32)],
        compiler_params=PARAMS,
        cost_estimate=pl.CostEstimate(flops=100_000, bytes_accessed=150_000, transcendentals=0),
        name="block_sum",
    )(came)


def last_sum_body(*refs):
    total = refs[0][...].astype(jnp.float32)
    for ref in refs[1:-1]:
        total += ref[...].astype(jnp.float32)
    refs[-1][...] = total


def last_sum(came):
    return pl.pallas_call(
        last_sum_body,
        out_shape=jax.ShapeDtypeStruct((TILES, LANES), jnp.float32),
        in_specs=[VMEM] * len(came),
        out_specs=VMEM,
        compiler_params=PARAMS,
        cost_estimate=pl.CostEstimate(flops=100_000, bytes_accessed=80_000, transcendentals=0),
        name="last_sum",
    )(*came)


def shards(sources, targets):
    blk = lax.axis_size("blk")
    own = gathered(sources)
    partial = exchange_term(own, from_ahead(own), gathered(targets))
    groups = [[part * BLOCK + i for i in range(BLOCK)] for part in range(PARTS)]
    came = lax.all_to_all(partial, "wide", split_axis=0, concat_axis=0, axis_index_groups=groups, tiled=True)
    sent = block_sum(came.reshape(BLOCK, PARTS * TILES, LANES))
    arrived = []
    for turn, ends in enumerate(ROUNDS):
        pairs = [(start * BLOCK + i, end * BLOCK + i) for start, end in ends.items() for i in range(BLOCK)]
        route = [(near * blk + b, far * blk + (b + 1) % blk) for near, far in pairs for b in range(blk)]
        arrived.append(lax.ppermute(sent[turn], ("wide", "blk"), route))
    return last_sum(arrived).reshape(1, -1)[:, :PIECE]


def solution(mesh):
    in_specs = (P(("wide", "blk"), None), P("blk", None))
    return jax.shard_map(shards, mesh=mesh, in_specs=in_specs, out_specs=P("blk", "wide"), check_vma=False)
```
